128 devices in a mesh: expert: 32 (over y, z, core), vocab: 4 (over x).
Axes of the slice: x: 4, y: 4, z: 4, core: 2. Of those that a mesh axis runs over, the one named last changes fastest.
Arguments:
- tokens: bfloat16 [4096, 2048], P('expert'), may hold values from -12 to 12
- expert_ids: int32 [4096, 6], P('expert'), may hold values from 0 to 63, all different within a row; in each aligned block of 128 rows (0 to 127, 128 to 255, ...) at most 24 rows name the same one
- gates: float32 [4096, 6], P('expert'), may hold values from 0.05 to 0.4
- w_gate: bfloat16 [64, 2048, 1408], P('expert', None, 'vocab'), may hold values from -0.125 to 0.125
- w_up: bfloat16 [64, 2048, 1408], P('expert', None, 'vocab'), may hold values from -0.125 to 0.125
- w_down: bfloat16 [64, 1408, 2048], P('expert', 'vocab'), may hold values from -0.21875 to 0.21875
- norm_gain: float32 [2048], replicated, may hold values from 0.5 to 1.5
- lm_weight: bfloat16 [2048, 98304], P(None, ('expert', 'vocab')), may hold values from -6.9605824 to 6.9605824
- targets: int32 [4096], P('expert'), may hold values from 0 to 98303
Outputs:
- logprobs: float32 [4096], P('expert')
The draws below stay inside these ranges and needn't reach their ends.
Inputs may be any that keep to these rules, and one draw needn't show every extreme that they name: `expert_ids`: in the 128 rows of one device no expert is named by more than 24 routes; each row names 6 different experts.
All inputs are finite; a program needn't handle non-finite values.
Results may differ from the reference program's by a relative error of at most 0.003.
Values may be sent and summed in bfloat16 or wider, within the bound.
A program may use at most 128 MiB of HBM per device.

```python
import math
import jax
import jax.numpy as jnp
import numpy as np
from jax import lax

D = 2048
FF = 1408
TOP = 6
TOK_DEV = 128
EXPERTS = 64
TOKENS = 4096
VOCAB = 98304
CAP = 24
N_EXPERT = 32


def draw_tokens(key, part):
    first_key = jax.random.fold_in(jax.random.fold_in(key, 11), 0)
    column = jnp.arange(D, dtype=jnp.float32)
    col_scale = 0.6 + 1.2 * column / D
    values = jnp.clip(jax.random.normal(first_key, (TOKENS, D), jnp.float32), -6.0, 6.0)
    return (values * col_scale[None, :]).astype(jnp.bfloat16)


def draw_lm_weight(key, part):
    inner_key = jax.random.fold_in(key, 23)
    values = jnp.clip(jax.random.normal(inner_key, (D, VOCAB), jnp.float32), -6.0, 6.0)
    return (values * 6.0 / jnp.sqrt(jnp.float32(D))).astype(jnp.bfloat16)


def plant(drawn, stream_key, least, largest):
    longest = drawn.shape.index(max(drawn.shape))
    spots = []
    for shift in (0, 1):
        where = [jax.random.randint(jax.random.fold_in(stream_key, axis), (), 0, length) for axis, length in enumerate(drawn.shape)]
        where[longest] = (where[longest] + shift) % drawn.shape[longest]
        spots.append(tuple(where))
    return drawn.at[spots[0]].set(least).at[spots[1]].set(largest)


def spiked(result, rng, source, target, parts, factor):
    owner, partner = [(jnp.arange(result.shape[dim]) // (result.shape[dim] // parts)).reshape([-1 if axis == dim else 1 for axis in range(result.ndim)]) for dim in (source, target)]
    chosen = jax.random.permutation(rng, parts)[partner]
    strong = (owner == chosen) | (owner == (partner + parts // 2) % parts)
    return jnp.where(strong, factor * result, result)


def shard_levels(rng, dims, cuts, smallest, largest):
    def one(dim, shards_of):
        steps = jax.random.uniform(jax.random.fold_in(jax.random.fold_in(rng, 6), dim), (shards_of,), jnp.float32, smallest / len(cuts), largest / len(cuts))
        return jnp.repeat(jnp.exp(steps), dims[dim] // shards_of).reshape((-1,) + (1,) * (len(dims) - dim - 1))

    loudness = one(*cuts[0])
    for cut in cuts[1:]:
        loudness = loudness * one(*cut)
    return loudness


def deal_out(key, own, number, rows, count, top, most, lean):
    order = jax.random.permutation(key, count)
    heavy_load, ordinary = shares(count, rows * top, most, lean, True), shares(count, rows * top, most, lean, False)
    places = jnp.arange(count)

    def named(lengths, rotation):
        used = int((lengths > 0).sum())
        fixed = max(1, used // 4)
        passed = fixed + (places - fixed + rotation * (used - fixed)) % max(1, count - fixed)
        return jnp.zeros((count,), jnp.int32).at[order[jnp.where(places < fixed, places, passed)]].set(jnp.asarray(lengths, jnp.int32))

    lengths = jnp.where(number % 4 == 0, named(heavy_load, number // 4), named(ordinary, number - number // 4 - 1))
    mixed = jax.random.permutation(jax.random.fold_in(own, 3), count)
    donor, receiver = mixed[0:count // 2 * 2:2], mixed[1:count // 2 * 2:2]
    slack = jnp.minimum(lengths[donor] - 1, most - lengths[receiver]) // 2
    slack = jnp.where((donor == order[0]) | (receiver == order[0]) | (lengths[receiver] == 0), 0, jnp.maximum(slack, 0))
    passed = jax.random.randint(jax.random.fold_in(own, 4), (count // 2,), 0, 1 << 20) % (slack + 1)
    lengths = lengths.at[donor].add(-passed).at[receiver].add(passed)
    members = jnp.searchsorted(jnp.cumsum(lengths), jnp.arange(rows * top), side="right").astype(jnp.int32)
    listing = members.reshape(top, rows).T
    listing = listing[jax.random.permutation(jax.random.fold_in(own, 1), rows)]
    rotation = jax.random.randint(jax.random.fold_in(own, 2), (rows, 1), 0, top)
    return jnp.take_along_axis(listing, (jnp.arange(top)[None, :] + rotation) % top, axis=1)


def shares(number_of, total, limit, skew, full):
    weights = [(1 << 20) // math.isqrt(grade ** skew) + 1 for grade in range(1, number_of + 1)]
    largest = limit if full else min(limit, max(-(-total // number_of), total * weights[0] // sum(weights)))
    least = 1 if total - largest >= number_of - 1 else 0
    counts, surplus = [largest] + [least] * (number_of - 1), total - largest - least * (number_of - 1)
    while surplus > 0:
        free = [i for i in range(1, number_of) if counts[i] < largest] or [i for i in range(1, number_of) if counts[i] < limit]
        whole, remaining = sum([weights[i] for i in free]), surplus
        for i in free:
            more = min(limit - counts[i], max(1, remaining * weights[i] // whole), surplus)
            counts[i] = counts[i] + more
            surplus = surplus - more
    return np.array(counts)


def scatter_about(stream_key, dims, scale, reach, shards=(), kind=jnp.bfloat16):
    loudness = shard_levels(stream_key, dims, shards, -0.22, 0.18) if shards else 1.0
    values = jax.random.normal(stream_key, dims, jnp.float32) * scale * loudness
    return jnp.minimum(jnp.maximum(values, -reach), reach).astype(kind)


def heavy_noise(key, extent, spread, reach, pieces, heavy, kind=jnp.bfloat16):
    array = spread * jax.random.normal(key, extent, jnp.float32)
    if pieces:
        array = array * shard_levels(key, extent, pieces, -0.22, 0.18)
    return jnp.clip(spiked(array, jax.random.fold_in(key, 3), *heavy), -reach, reach).astype(kind)


def setup_inputs(seed: int = 0) -> dict:
    keys = jax.random.split(jax.random.key(seed), 10)
    tokens = draw_tokens(jax.random.fold_in(keys[9], 71), 0)
    expert_ids_keys = jax.random.split(jax.random.fold_in(keys[1], 1), TOKENS // TOK_DEV)
    expert_ids_turns = jax.random.permutation(jax.random.fold_in(keys[1], 3), TOKENS // TOK_DEV)
    expert_ids = jax.vmap(lambda own, number: deal_out(jax.random.fold_in(keys[1], 2), own, number, TOK_DEV, EXPERTS, TOP, CAP, 2))(expert_ids_keys, expert_ids_turns).reshape((TOKENS, TOP))
    gates = jnp.clip(jnp.exp(math.log(0.4) - 2.0794415 * jax.random.uniform(keys[2], (TOKENS, TOP), jnp.float32) ** shard_levels(keys[2], (TOKENS, TOP), ((0, 32),), -0.2, 0.2)), 0.05, 0.4)
    w_gate = scatter_about(keys[3], (EXPERTS, D, FF), D ** -0.5, 0.125, ((0, 32), (2, 4)))
    w_up = scatter_about(keys[4], (EXPERTS, D, FF), D ** -0.5, 0.125, ((0, 32), (2, 4)))
    w_down = heavy_noise(keys[5], (EXPERTS, FF, D), FF ** -0.5, 0.21875, ((0, 32), (1, 4)), (1, 2, 4, 2.0))
    norm_gain = jnp.clip(1.0 + 0.1 * jax.random.normal(keys[6], (D,), jnp.float32), 0.5, 1.5)
    lm_weight = draw_lm_weight(jax.random.fold_in(keys[9], 71), 0)
    targets = plant(jax.random.randint(keys[8], (TOKENS,), 0, VOCAB), jax.random.fold_in(keys[8], 1), 0, VOCAB - 1).astype(jnp.int32)
    return {"tokens": tokens, "expert_ids": expert_ids, "gates": gates, "w_gate": w_gate, "w_up": w_up, "w_down": w_down, "norm_gain": norm_gain, "lm_weight": lm_weight, "targets": targets}


def expert_ffn(rows, gate_mat, up_mat, down_mat):
    gate_val = jnp.dot(rows, gate_mat, preferred_element_type=jnp.float32)
    up_val = jnp.dot(rows, up_mat, preferred_element_type=jnp.float32)
    hidden = (jax.nn.silu(gate_val) * up_val).astype(jnp.bfloat16)
    return jnp.dot(hidden, down_mat, preferred_element_type=jnp.float32)

def reference(tokens, expert_ids, gates, w_gate, w_up, w_down, norm_gain, lm_weight, targets):
    sources = N_EXPERT
    block_ids = expert_ids.reshape(sources, TOK_DEV * TOP).astype(jnp.int32)
    onehot = (block_ids[:, :, None] == jnp.arange(EXPERTS, dtype=jnp.int32)[None, None, :]).astype(jnp.int32)
    slot_ids = lax.optimization_barrier(jnp.sum((jnp.cumsum(onehot, axis=1) - onehot) * onehot, axis=2))
    flat_expert = block_ids.reshape(-1)
    flat_source = jnp.repeat(jnp.arange(sources, dtype=jnp.int32), TOK_DEV * TOP)
    flat_token = jnp.repeat(jnp.arange(TOKENS, dtype=jnp.int32), TOP)
    flat_place = flat_source * CAP + slot_ids.reshape(-1).astype(jnp.int32)
    buffer = jnp.zeros((EXPERTS, sources * CAP, D), tokens.dtype).at[flat_expert, flat_place].set(tokens[flat_token])
    outputs = lax.map(lambda item: expert_ffn(item[0], item[1], item[2], item[3]), (buffer, w_gate, w_up, w_down))
    picked = outputs[flat_expert, flat_place].reshape(TOKENS, TOP, D)
    mixture = lax.optimization_barrier(jnp.sum(picked * gates[:, :, None].astype(jnp.float32), axis=1))
    resid = (tokens.astype(jnp.float32) + mixture).astype(jnp.bfloat16)
    resid_f = resid.astype(jnp.float32)
    squares = lax.optimization_barrier(jnp.mean(resid_f * resid_f, axis=1))
    normed = (resid_f * lax.rsqrt(squares + 1e-06)[:, None] * norm_gain[None, :]).astype(jnp.bfloat16)
    width_block = math.gcd(VOCAB, 8192)
    blocks = VOCAB // width_block
    weight_blocks = lm_weight.reshape(D, blocks, width_block).transpose(1, 0, 2)

    def sweep(carry, item):
        best, mass, chosen = carry
        block_w, index = item
        logits = jnp.dot(normed, block_w, preferred_element_type=jnp.float32)
        new_best = jnp.maximum(best, lax.optimization_barrier(jnp.max(logits, axis=1)))
        mass = mass * jnp.exp(best - new_best) + lax.optimization_barrier(jnp.sum(jnp.exp(logits - new_best[:, None]), axis=1))
        cols = index * width_block + jnp.arange(width_block, dtype=jnp.int32)
        chosen = chosen + lax.optimization_barrier(jnp.sum(jnp.where(cols[None, :] == targets[:, None], logits, 0.0), axis=1))
        return ((new_best, mass, chosen), None)
    start = (jnp.full((TOKENS,), -1e+30, jnp.float32), jnp.zeros((TOKENS,), jnp.float32), jnp.zeros((TOKENS,), jnp.float32))
    (best, mass, chosen), _ = lax.scan(sweep, start, (weight_blocks, jnp.arange(blocks, dtype=jnp.int32)))
    return chosen - best - jnp.log(mass)
```

```python
import jax
import jax.numpy as jnp
from jax import lax
from jax.experimental import pallas as pl
from jax.experimental.pallas import tpu as pltpu
from jax.sharding import PartitionSpec as P

MESH = pl.DeviceIdType.MESH
BF = jnp.bfloat16
F32 = jnp.float32
COLORS = (("x", "y", "z", 0, 768), ("y", "z", "x", 768, 640), ("z", "x", "y", 1408, 640))


def coords():
    e = lax.axis_index("expert")
    return {"x": lax.axis_index("vocab"), "y": e // 8, "z": (e // 2) % 4, "c": e % 2}


def device(co, **changed):
    q = dict(co, **changed)
    return {"expert": (q["y"] * 4 + q["z"]) * 2 + q["c"], "vocab": q["x"]}


def shift(co, dim, by):
    return (co[dim] + by) % 4


def view(buf, idx, cols, half=None):
    rows = slice(None) if half is None else pl.ds(16 * half, 16)
    y, z, x = (pl.ds(0, 4) if idx[d] is None else idx[d] for d in "yzx")
    return buf.at[y, z, x, rows, pl.ds(cols[0], cols[1])]


def remote(src, dst, ssem, rsem, to):
    return pltpu.make_async_remote_copy(src, dst, ssem, rsem, device_id=to, device_id_type=MESH)


class GatherRing:
    def __init__(self, buf, co, dim, idx, cols, ssem, rsem):
        self.buf, self.co, self.dim, self.idx, self.cols = buf, co, dim, idx, cols
        self.ssem, self.rsem = ssem, rsem
        self.left, self.right = shift(co, dim, -1), shift(co, dim, 1)
        self.far, self.me = shift(co, dim, 2), co[dim]

    def copy(self, n, k, half, to):
        ref = view(self.buf, dict(self.idx, **{self.dim: k}), self.cols, half)
        return remote(ref, ref, self.ssem.at[n], self.rsem.at[n], device(self.co, **{self.dim: to}))

    def start(self):
        self.copy(0, self.me, None, self.right).start()
        self.copy(1, self.me, None, self.left).start()

    def forward(self):
        self.copy(0, self.left, None, self.right).wait_recv()
        self.copy(2, self.left, 0, self.right).start()
        self.copy(1, self.right, None, self.left).wait_recv()
        self.copy(3, self.right, 1, self.left).start()

    def forward_left(self):
        self.copy(0, self.left, None, self.right).wait_recv()
        self.copy(2, self.left, 0, self.right).start()

    def forward_right(self):
        self.copy(1, self.right, None, self.left).wait_recv()
        self.copy(3, self.right, 1, self.left).start()

    def finish(self):
        self.copy(2, self.far, 0, self.right).wait_recv()
        self.copy(3, self.far, 1, self.left).wait_recv()

    def drain(self):
        self.copy(0, self.me, None, self.right).wait_send()
        self.copy(1, self.me, None, self.left).wait_send()
        self.copy(2, self.left, 0, self.right).wait_send()
        self.copy(3, self.right, 1, self.left).wait_send()


def gather_all(buf, co, ssem, rsem):
    first, second, third = [], [], []
    for n, (a, b, c, lo, width) in enumerate(COLORS):
        base = {d: co[d] for d in "xyz"}
        first.append(GatherRing(buf, co, a, base, (lo, width), ssem.at[n, 0], rsem.at[n, 0]))
        line = dict(base, **{a: None})
        second.append(GatherRing(buf, co, b, line, (lo, width), ssem.at[n, 1], rsem.at[n, 1]))
        third.append(
            [
                GatherRing(buf, co, c, dict(line, **{b: shift(co, b, k)}), (lo, width), ssem.at[n, 2 + j], rsem.at[n, 2 + j])
                for j, k in enumerate((0, -1, 1, 2))
            ]
        )
    three = range(3)
    for n in three:
        first[n].start()
    for n in three:
        first[n].forward()
    for n in three:
        first[n].finish()
        second[n].start()
        third[n][0].start()
    for n in three:
        second[n].forward_left()
        third[n][1].start()
        second[n].forward_right()
        third[n][2].start()
    for n in three:
        third[n][0].forward()
    for n in three:
        second[n].finish()
        third[n][3].start()
    for j in (1, 2):
        for n in three:
            third[n][j].forward()
    for n in three:
        third[n][0].finish()
    for n in three:
        third[n][3].forward()
    for j in (1, 2, 3):
        for n in three:
            third[n][j].finish()
    for n in three:
        for ring in [first[n], second[n]] + third[n]:
            ring.drain()


class ScatterRing:
    def __init__(self, acc, land, co, dim, idx, cols, ssem, rsem):
        self.acc, self.co, self.dim, self.idx, self.cols = acc, co, dim, idx, cols
        self.land, self.ssem, self.rsem = land, ssem, rsem
        self.left, self.right = shift(co, dim, -1), shift(co, dim, 1)
        self.far, self.me = shift(co, dim, 2), co[dim]

    def piece(self, k, half=None):
        return view(self.acc, dict(self.idx, **{self.dim: k}), self.cols, half)

    def landing(self, n):
        cols = pl.ds(self.cols[0], self.cols[1])
        full = [slice(None)] * (len(self.land.shape) - 3)
        if n < 2:
            return self.land.at[(0, *full, pl.ds(16 * n, 16), cols)]
        return self.land.at[(n - 1, *full, slice(None), cols)]

    def copy(self, n, src, to):
        return remote(src, self.landing(n), self.ssem.at[n], self.rsem.at[n], device(self.co, **{self.dim: to}))

    def add(self, k, half, n):
        at, got = self.piece(k, half), self.landing(n)
        at[...] = (at[...].astype(F32) + got[...].astype(F32)).astype(BF)

    def start(self):
        self.copy(0, self.piece(self.far, 0), self.left).start()
        self.copy(1, self.piece(self.far, 1), self.right).start()

    def forward(self):
        self.copy(0, self.piece(self.left, 0), self.left).wait_recv()
        self.add(self.left, 0, 0)
        self.copy(2, self.piece(self.left), self.left).start()
        self.copy(1, self.piece(self.right, 1), self.right).wait_recv()
        self.add(self.right, 1, 1)
        self.copy(3, self.piece(self.right), self.right).start()

    def finish(self):
        self.copy(2, self.piece(self.me), self.left).wait_recv()
        self.add(self.me, None, 2)
        self.copy(3, self.piece(self.me), self.right).wait_recv()
        self.add(self.me, None, 3)

    def drain(self):
        self.copy(0, self.piece(self.far, 0), self.left).wait_send()
        self.copy(1, self.piece(self.far, 1), self.right).wait_send()
        self.copy(2, self.piece(self.left), self.left).wait_send()
        self.copy(3, self.piece(self.right), self.right).wait_send()


def scatter_all(acc, land_c, land_b, land_a, co, ssem, rsem):
    first, second, third = [], [], []
    for n, (a, b, c, lo, width) in enumerate(COLORS):
        base = {d: co[d] for d in "xyz"}
        cols = (lo, width)
        line = dict(base, **{a: None})
        first.append(
            [
                ScatterRing(acc, land_c.at[j], co, c, dict(line, **{b: shift(co, b, k)}), cols, ssem.at[n, j], rsem.at[n, j])
                for j, k in enumerate((2, -1, 1, 0))
            ]
        )
        second.append(ScatterRing(acc, land_b, co, b, line, cols, ssem.at[n, 4], rsem.at[n, 4]))
        third.append(ScatterRing(acc, land_a, co, a, base, cols, ssem.at[n, 5], rsem.at[n, 5]))
    three = range(3)
    for j in range(4):
        for n in three:
            first[n][j].start()
    for j in range(4):
        for n in three:
            first[n][j].forward()
    for n in three:
        first[n][0].finish()
        second[n].start()
    for j in (1, 2):
        for n in three:
            first[n][j].finish()
    for n in three:
        second[n].forward()
    for n in three:
        first[n][3].finish()
    for n in three:
        second[n].finish()
        third[n].start()
    for n in three:
        third[n].forward()
    for n in three:
        third[n].finish()
    for n in three:
        for ring in first[n] + [second[n], third[n]]:
            ring.drain()


def greet(barrier, to):
    pl.semaphore_signal(barrier, inc=1, device_id=to, device_id_type=MESH)


def greet_neighbours(co, barrier):
    for dim in "xyz":
        for by in (1, -1):
            greet(barrier, device(co, **{dim: shift(co, dim, by)}))
    greet(barrier, device(co, c=1 - co["c"]))


def plane_peer(co, r):
    q = (co["y"] * 4 + co["z"] + r) % 16
    return device(co, y=q // 4, z=q % 4)


def experts_kernel(
    tok, info, wg, wu, wd, part, info_all,
    buf, vg, vu, vd, rows, picks, row_gate, masks, gates, places,
    ssem, rsem, isend, irecv, wsend, wrecv, local,
):
    co = coords()
    q_me = co["y"] * 4 + co["z"]
    barrier = pltpu.get_barrier_semaphore()
    greet_neighbours(co, barrier)
    for r in range(1, 16):
        greet(barrier, plane_peer(co, r))
    own = pltpu.make_async_copy(
        tok.at[pl.ds(pl.multiple_of(co["x"] * 32, 32), 32)], buf.at[co["y"], co["z"], co["x"]], local.at[0]
    )
    own.start()
    mine = pl.ds(co["c"] * 2, 2)
    pairs = ((wg, vg), (wu, vu), (wd, vd))
    weights = [pltpu.make_async_copy(src, dst.at[mine], local.at[1 + i]) for i, (src, dst) in enumerate(pairs)]
    for w in weights:
        w.start()
    info_all[0] = info[...]
    own.wait()
    pl.semaphore_wait(barrier, 22)
    swaps = [
        remote(src, dst.at[mine], wsend.at[i], wrecv.at[i], device(co, c=1 - co["c"])) for i, (src, dst) in enumerate(pairs)
    ]
    notes = [remote(info, info_all.at[r], isend.at[r], irecv.at[r], plane_peer(co, r)) for r in range(1, 16)]
    for n in notes:
        n.start()
    for s in swaps:
        s.start()
    gather_all(buf, co, ssem, rsem)
    for n in notes:
        n.wait()

    def read_source(q, _):
        got = info_all[(q_me - q + 16) % 16]
        ids, weight = got[0:6], got[8:14]
        mask_rows, gate_rows = [], []
        for l in range(4):
            hit = ids == (4 * q_me + l).astype(F32)
            mask_rows.append(jnp.sum(jnp.where(hit, 1.0, 0.0), axis=0, keepdims=True))
            gate_rows.append(jnp.sum(jnp.where(hit, weight, 0.0), axis=0, keepdims=True))
        zero = jnp.zeros((4, 128), F32)
        at = pl.ds(pl.multiple_of(q * 8, 8), 8)
        masks[at] = jnp.concatenate(mask_rows + [zero], axis=0)
        gates[at] = jnp.concatenate(gate_rows + [zero], axis=0)
        return 0

    lax.fori_loop(0, 16, read_source, 0)
    before = (
        lax.broadcasted_iota(jnp.int32, (128, 128), 0) < lax.broadcasted_iota(jnp.int32, (128, 128), 1)
    ).astype(F32).astype(BF)
    taken = masks[...]
    ahead = jnp.dot(taken.astype(BF), before, preferred_element_type=F32)
    places[...] = jnp.where(taken > 0.0, ahead, -1.0)

    def select(p, _):
        slot = lax.broadcasted_iota(jnp.int32, (24, 128), 0).astype(F32)
        zero = jnp.zeros((24, 128), F32)
        at = pl.ds(pl.multiple_of(p * 16, 16), 16)
        place, weight = places[at], gates[at]
        out = []
        for l in range(4):
            for s in range(2):
                k = s * 8 + l
                hit = jnp.where(place[k : k + 1] == slot, 1.0, 0.0)
                out.append(jnp.concatenate([hit, zero] if s == 0 else [zero, hit], axis=1))
                row_gate[l, pl.ds(pl.multiple_of(p * 48 + s * 24, 8), 24)] = jnp.sum(
                    hit * weight[k : k + 1], axis=1, keepdims=True
                )
        pick = jnp.concatenate(out, axis=0).astype(BF)
        picks[p] = pick
        two = buf[p // 2, pl.ds((p % 2) * 2, 2)].reshape(256, 2048)
        got = jnp.dot(pick, two, preferred_element_type=F32).astype(BF)
        for l in range(4):
            rows[l, pl.ds(pl.multiple_of(p * 48, 16), 48)] = got[l * 48 : (l + 1) * 48]
        return 0

    lax.fori_loop(0, 8, select, 0)
    for w in weights:
        w.wait()
    for s in swaps:
        s.wait()

    def ffn(l, _):
        got = rows[l]
        gate = jnp.dot(got, vg[l], preferred_element_type=F32)
        up = jnp.dot(got, vu[l], preferred_element_type=F32)
        hidden = (gate / (1.0 + jnp.exp(-gate)) * up).astype(BF)
        rows[l] = (jnp.dot(hidden, vd[l], preferred_element_type=F32) * row_gate[l]).astype(BF)
        return 0

    lax.fori_loop(0, 4, ffn, 0)

    def combine(p, _):
        at = pl.ds(pl.multiple_of(p * 48, 16), 48)
        got = jnp.concatenate([rows[l, at] for l in range(4)], axis=0)
        mixed = lax.dot_general(picks[p], got, (((0,), (0,)), ((), ())), preferred_element_type=F32)
        part[p // 2, pl.ds((p % 2) * 2, 2)] = mixed.astype(BF).reshape(2, 4, 32, 2048)
        return 0

    lax.fori_loop(0, 8, combine, 0)


def head_kernel(
    part, tok, gain, lm, targets, out,
    acc, land_c, land_b, land_a, buf, words, mine, stats, got,
    sc_send, sc_recv, ga_send, ga_recv, st_send, st_recv, wsend, wrecv, local,
):
    co = coords()
    q_me = co["y"] * 4 + co["z"]
    u_me = q_me * 4 + co["x"]
    barrier = pltpu.get_barrier_semaphore()
    greet_neighbours(co, barrier)
    load = pltpu.make_async_copy(part, acc, local.at[0])
    load.start()
    words_in = pltpu.make_async_copy(lm, words.at[co["c"]], local.at[1])
    words_in.start()
    own = pltpu.make_async_copy(tok.at[pl.ds(pl.multiple_of(co["x"] * 32, 32), 32)], mine, local.at[2])
    own.start()
    load.wait()
    own.wait()
    pl.semaphore_wait(barrier, 7)
    scatter_all(acc, land_c, land_b, land_a, co, sc_send, sc_recv)
    swap = remote(lm, words.at[co["c"]], wsend, wrecv, device(co, c=1 - co["c"]))
    swap.start()
    resid = (mine[...].astype(F32) + acc[co["y"], co["z"], co["x"]].astype(F32)).astype(BF).astype(F32)
    square = jnp.mean(resid * resid, axis=1, keepdims=True)
    buf[co["y"], co["z"], co["x"]] = (resid * lax.rsqrt(square + 1e-06) * gain[...]).astype(BF)
    gather_all(buf, co, ga_send, ga_recv)
    words_in.wait()
    swap.wait()
    lane = lax.broadcasted_iota(jnp.int32, (128, 128), 1)

    def head(p, _):
        two = buf[p // 2, pl.ds((p % 2) * 2, 2)].reshape(256, 2048)
        goal = []
        for s in range(2):
            row = targets[(q_me - (2 * p + s) + 16) % 16][14:15]
            goal.append(jnp.transpose(jnp.broadcast_to(row, (128, 128)))[:, 0:1])
        goal = jnp.concatenate(goal, axis=0).astype(jnp.int32)
        tops, logits = [], []
        for c in range(2):
            value = jnp.dot(two, words[c], preferred_element_type=F32)
            logits.append(value)
            tops.append(jnp.max(value, axis=1, keepdims=True))
        top = jnp.maximum(*tops)
        total, chosen = 0.0, 0.0
        for c in range(2):
            base = ((q_me * 2 + c) * 4 + co["x"]) * 768
            total += jnp.sum(jnp.exp(logits[c] - top), axis=1, keepdims=True)
            column = lax.broadcasted_iota(jnp.int32, (256, 768), 1)
            chosen += jnp.sum(jnp.where(column == goal - base, logits[c], 0.0), axis=1, keepdims=True)
        norm = top + jnp.log(total)
        for s in range(2):
            at = slice(s * 128, (s + 1) * 128)
            both = jnp.where(lane == 0, norm[at], jnp.where(lane == 1, chosen[at], 0.0))
            stats[2 * p + s] = jnp.transpose(both)[0:2]
        return 0

    lax.fori_loop(0, 8, head, 0)

    def note(r):
        u = (u_me + r) % 64
        q = u // 4
        to = device(co, y=q // 4, z=q % 4, x=u % 4)
        return remote(stats.at[q], got.at[r], st_send.at[r], st_recv.at[r], to)

    def send(r, _):
        note(r).start()
        return 0

    def wait(r, _):
        note(r).wait()
        return 0

    lax.fori_loop(1, 64, send, 0)
    got[0] = stats[q_me]
    lax.fori_loop(1, 64, wait, 0)
    norms = got[:, 0, :]
    best = jnp.max(norms, axis=0, keepdims=True)
    mass = jnp.sum(jnp.exp(norms - best), axis=0, keepdims=True)
    chosen = jnp.sum(got[:, 1, :], axis=0, keepdims=True)
    out[...] = chosen - best - jnp.log(mass)


def vmem(*shape, dtype=BF):
    return pltpu.VMEM(shape, dtype)


def body(tokens, expert_ids, gates, w_gate, w_up, w_down, norm_gain, lm_weight, targets):
    info = jnp.concatenate(
        [
            expert_ids.astype(F32).T,
            jnp.zeros((2, 128), F32),
            gates.T,
            targets.astype(F32)[None],
            jnp.zeros((1, 128), F32),
        ],
        axis=0,
    )
    hbm, chip = pl.BlockSpec(memory_space=pl.ANY), pl.BlockSpec(memory_space=pltpu.VMEM)
    dma = pltpu.SemaphoreType.DMA
    part, info_all = pl.pallas_call(
        experts_kernel,
        out_shape=(jax.ShapeDtypeStruct((4, 4, 4, 32, 2048), BF), jax.ShapeDtypeStruct((16, 16, 128), F32)),
        in_specs=[hbm, chip, hbm, hbm, hbm],
        out_specs=(chip, chip),
        scratch_shapes=[
            vmem(4, 4, 4, 32, 2048), vmem(4, 2048, 352), vmem(4, 2048, 352), vmem(4, 352, 2048),
            vmem(4, 384, 2048), vmem(8, 192, 256), vmem(4, 384, 1, dtype=F32),
            vmem(128, 128, dtype=F32), vmem(128, 128, dtype=F32), vmem(128, 128, dtype=F32),
            dma((3, 6, 4)), dma((3, 6, 4)), dma((16,)), dma((16,)), dma((3,)), dma((3,)), dma((4,)),
        ],
        compiler_params=pltpu.CompilerParams(collective_id=0, has_side_effects=True, vmem_limit_bytes=63 << 20),
        name="experts",
    )(tokens, info, w_gate, w_up, w_down)
    out = pl.pallas_call(
        head_kernel,
        out_shape=jax.ShapeDtypeStruct((1, 128), F32),
        in_specs=[hbm, hbm, chip, hbm, chip],
        out_specs=chip,
        scratch_shapes=[
            vmem(4, 4, 4, 32, 2048), vmem(4, 3, 4, 32, 2048), vmem(3, 4, 32, 2048), vmem(3, 32, 2048),
            vmem(4, 4, 4, 32, 2048), vmem(2, 2048, 768), vmem(32, 2048),
            vmem(16, 2, 128, dtype=F32), vmem(64, 2, 128, dtype=F32),
            dma((3, 6, 4)), dma((3, 6, 4)), dma((3, 6, 4)), dma((3, 6, 4)), dma((64,)), dma((64,)), dma, dma, dma((3,)),
        ],
        compiler_params=pltpu.CompilerParams(collective_id=1, has_side_effects=True, vmem_limit_bytes=63 << 20),
        name="head",
    )(part, tokens, norm_gain[None], lm_weight, info_all)
    return out[0]


def solution(mesh):
    in_specs = (
        P("expert", None),
        P("expert", None),
        P("expert", None),
        P("expert", None, "vocab"),
        P("expert", None, "vocab"),
        P("expert", "vocab", None),
        P(),
        P(None, ("expert", "vocab")),
        P("expert"),
    )
    return jax.shard_map(body, mesh=mesh, in_specs=in_specs, out_specs=P("expert"), check_vma=False)
```

```python
import jax
import jax.numpy as jnp
from jax import lax
from jax.experimental import pallas as pl
from jax.experimental.pallas import tpu as pltpu
from jax.sharding import PartitionSpec as P

MESH = pl.DeviceIdType.MESH
BF = jnp.bfloat16
F32 = jnp.float32
COLORS = (("x", "y", "z", 0, 768), ("z", "y", "x", 768, 768), ("x", "z", "y", 1536, 512))
BACK = (("x", "y", "z", 0, 768), ("z", "y", "x", 768, 896), ("x", "z", "y", 1664, 384))
GROUPS = (0, -1, 1, 2)
OWN, LEFT, RIGHT, FAR = range(4)


def coords():
    e = lax.axis_index("expert")
    return {"x": lax.axis_index("vocab"), "y": e // 8, "z": (e // 2) % 4, "c": e % 2}


def device(co, **changed):
    q = dict(co, **changed)
    return {"expert": (q["y"] * 4 + q["z"]) * 2 + q["c"], "vocab": q["x"]}


def shift(co, dim, by):
    return (co[dim] + by) % 4


def view(buf, idx, cols, half=None):
    rows = slice(None) if half is None else pl.ds(16 * half, 16)
    y, z, x = (pl.ds(0, 4) if idx[d] is None else idx[d] for d in "yzx")
    return buf.at[y, z, x, rows, pl.ds(cols[0], cols[1])]


def remote(src, dst, ssem, rsem, to):
    return pltpu.make_async_remote_copy(src, dst, ssem, rsem, device_id=to, device_id_type=MESH)


class GatherRing:
    def __init__(self, buf, co, dim, idx, cols, ssem, rsem):
        self.buf, self.co, self.dim, self.idx, self.cols = buf, co, dim, idx, cols
        self.ssem, self.rsem = ssem, rsem
        self.left, self.right = shift(co, dim, -1), shift(co, dim, 1)
        self.far, self.me = shift(co, dim, 2), co[dim]

    def copy(self, n, k, half, to):
        ref = view(self.buf, dict(self.idx, **{self.dim: k}), self.cols, half)
        return remote(ref, ref, self.ssem, self.rsem.at[n], device(self.co, **{self.dim: to}))

    def start(self):
        self.copy(0, self.me, None, self.right).start()
        self.copy(1, self.me, None, self.left).start()

    def forward(self):
        self.copy(0, self.left, None, self.right).wait_recv()
        self.copy(2, self.left, 0, self.right).start()
        self.copy(1, self.right, None, self.left).wait_recv()
        self.copy(2, self.right, 1, self.left).start()

    def finish(self):
        self.copy(2, self.far, None, self.right).wait_recv()


class GatherLine(GatherRing):
    def start(self):
        for n, to in enumerate((self.right, self.left, self.far)):
            self.copy(n, self.me, None, to).start()

    def finish(self):
        for n, k in enumerate((self.left, self.right, self.far)):
            self.copy(n, k, None, self.far).wait_recv()


def drain(buf, sems, colors, co, lines):
    for n, (_, _, _, lo, width) in enumerate(colors):
        cols = pl.ds(lo, width)
        sizes = (buf.at[0, 0, pl.ds(0, 3), :, cols], buf.at[pl.ds(0, 3), :, 0, :, cols], buf.at[pl.ds(0, 3), :, :, :, cols])
        for kind in range(3):
            if kind or n in lines:
                pltpu.make_async_copy(sizes[kind], sizes[kind], sems.at[n, kind]).wait()


def gather_groups(buf, co, ssem, rsem, have_x, idle, group):
    first, second, third = [], [], []
    for n, (a, b, c, lo, width) in enumerate(COLORS):
        base = {d: co[d] for d in "xyz"}
        first.append(GatherLine(buf, co, a, base, (lo, width), ssem.at[n, 0], rsem.at[n, 0]))
        line = dict(base, **{a: None})
        second.append(GatherRing(buf, co, b, line, (lo, width), ssem.at[n, 1], rsem.at[n, 1]))
        third.append(
            [
                GatherRing(buf, co, c, dict(line, **{b: shift(co, b, k)}), (lo, width), ssem.at[n, 2], rsem.at[n, 2 + j])
                for j, k in enumerate(GROUPS)
            ]
        )
    needed = [n for n in range(3) if not (have_x and COLORS[n][0] == "x")]
    ready = [n for n in range(3) if n not in needed]
    for n in needed:
        first[n].start()
    for n in ready:
        second[n].start()
    for n in ready:
        if n < 2:
            third[n][OWN].start()
    for n in needed:
        first[n].finish()
        second[n].start()
        if n < 2:
            third[n][OWN].start()
    third[2][OWN].start()
    for n in (0, 2):
        ring = second[n]
        ring.copy(0, ring.left, None, ring.right).wait_recv()
        ring.copy(2, ring.left, 0, ring.right).start()
        third[n][LEFT].start()
        ring.copy(1, ring.right, None, ring.left).wait_recv()
        ring.copy(2, ring.right, 1, ring.left).start()
        if n == 2:
            third[n][RIGHT].start()
    third[1][OWN].forward()
    third[0][OWN].forward()
    second[1].forward()
    third[1][LEFT].start()
    third[0][RIGHT].start()
    third[1][RIGHT].start()
    third[2][OWN].forward()
    for n in (0, 2, 1):
        second[n].finish()
    third[2][FAR].start()
    for n in (0, 1):
        third[n][LEFT].forward()
        third[n][FAR].start()
    for j in (LEFT, RIGHT):
        third[2][j].forward()
    idle()
    for n in (0, 1):
        third[n][OWN].finish()
    third[2][FAR].forward()
    group(OWN)
    for n in (0, 1):
        third[n][RIGHT].forward()
    for n in (0, 1):
        third[n][LEFT].finish()

    def far_on():
        for n in (0, 1):
            third[n][FAR].forward()

    group(LEFT, far_on)
    for n in (0, 1):
        third[n][RIGHT].finish()
    group(RIGHT)
    for n in (0, 1):
        third[n][FAR].finish()
    for j in range(4):
        third[2][j].finish()
    group(FAR)
    return needed


class ScatterRing:
    def __init__(self, acc, land, co, dim, idx, cols, ssem, rsem):
        self.acc, self.co, self.dim, self.idx, self.cols = acc, co, dim, idx, cols
        self.land, self.ssem, self.rsem = land, ssem, rsem
        self.left, self.right = shift(co, dim, -1), shift(co, dim, 1)
        self.far, self.me = shift(co, dim, 2), co[dim]

    def piece(self, k, half=None):
        return view(self.acc, dict(self.idx, **{self.dim: k}), self.cols, half)

    def landing(self, n):
        cols = pl.ds(self.cols[0], self.cols[1])
        full = [slice(None)] * (len(self.land.shape) - 3)
        if n < 2:
            return self.land.at[(0, *full, pl.ds(16 * n, 16), cols)]
        return self.land.at[(n - 1, *full, slice(None), cols)]

    def copy(self, n, src, to):
        sem = self.rsem.at[min(n, 2)]
        return remote(src, self.landing(n), self.ssem, sem, device(self.co, **{self.dim: to}))

    def add(self, k, half, *numbers):
        at, parts = self.piece(k, half), [self.landing(n) for n in numbers]
        if len(at.shape) == 2:
            total = at[...].astype(F32)
            for got in parts:
                total = total + got[...].astype(F32)
            at[...] = total.astype(BF)
        else:

            def one(i, _):
                total = at[i].astype(F32)
                for got in parts:
                    total = total + got[i].astype(F32)
                at[i] = total.astype(BF)
                return 0

            lax.fori_loop(0, at.shape[0], one, 0)

    def start(self):
        self.copy(0, self.piece(self.far, 0), self.left).start()
        self.copy(1, self.piece(self.far, 1), self.right).start()

    def forward(self):
        self.copy(0, self.piece(self.left, 0), self.left).wait_recv()
        self.add(self.left, 0, 0)
        self.copy(2, self.piece(self.left), self.left).start()
        self.copy(1, self.piece(self.right, 1), self.right).wait_recv()
        self.add(self.right, 1, 1)
        self.copy(3, self.piece(self.right), self.right).start()

    def finish(self):
        cols = pl.ds(self.cols[0], self.cols[1])
        full = [slice(None)] * (len(self.land.shape) - 2)
        both = self.land.at[(pl.ds(1, 2), *full, cols)]
        pltpu.make_async_copy(both, both, self.rsem.at[2]).wait()
        self.add(self.me, None, 2, 3)


class ScatterLine(ScatterRing):
    def copy(self, n, src, to):
        land = self.land.at[n, :, pl.ds(self.cols[0], self.cols[1])]
        return remote(src, land, self.ssem, self.rsem.at[n], device(self.co, **{self.dim: to}))

    def landing(self, n):
        return self.land.at[n, :, pl.ds(self.cols[0], self.cols[1])]

    def start(self):
        for n, to in enumerate((self.right, self.left, self.far)):
            self.copy(n, self.piece(to), to).start()

    def finish(self):
        for n in range(3):
            self.copy(n, self.piece(self.me), self.far).wait_recv()
        self.add(self.me, None, 0, 1, 2)


def scatter_rings(acc, land_c, land_b, land_a, co, ssem, rsem):
    first, second, third = [], [], []
    for n, (a, b, c, lo, width) in enumerate(BACK):
        base = {d: co[d] for d in "xyz"}
        cols = (lo, width)
        line = dict(base, **{a: None})
        first.append(
            [
                ScatterRing(acc, land_c.at[j], co, c, dict(line, **{b: shift(co, b, k)}), cols, ssem.at[n, 2], rsem.at[n, 2 + j])
                for j, k in enumerate(GROUPS)
            ]
        )
        second.append(ScatterRing(acc, land_b, co, b, line, cols, ssem.at[n, 1], rsem.at[n, 1]))
        third.append(ScatterLine(acc, land_a, co, a, base, cols, ssem.at[n, 0], rsem.at[n, 0]))
    return first, second, third


def greet(barrier, to):
    pl.semaphore_signal(barrier, inc=1, device_id=to, device_id_type=MESH)


def greet_neighbours(co, barrier):
    for dim in "xyz":
        for by in (1, -1):
            greet(barrier, device(co, **{dim: shift(co, dim, by)}))
    greet(barrier, device(co, c=1 - co["c"]))


def plane_peer(co, r):
    q = (co["y"] * 4 + co["z"] + r) % 16
    return device(co, y=q // 4, z=q % 4)


def kernel(
    tok, ids, weight, targets, wg, wu, wd, gain, lm, out,
    buf, vgu, vd, info, part, land_c, land_b, land_a, words, mine, goals, stats, got,
    rows, picks, row_gate, masks, gates, places,
    ga_send, ga_recv, sc_send, sc_recv, st_send, st_recv, isend, irecv, wsend, wrecv, local,
):
    co = coords()
    q_me = co["y"] * 4 + co["z"]
    sibling = device(co, c=1 - co["c"])
    barrier = pltpu.get_barrier_semaphore()
    greet_neighbours(co, barrier)

    def greet_peer(r, _):
        greet(barrier, plane_peer(co, r))
        return 0

    lax.fori_loop(1, 16, greet_peer, 0)
    shard = pl.ds(pl.multiple_of(co["x"] * 32, 32), 32)
    owns = []
    for n, (a, _, _, lo, width) in enumerate(COLORS):
        cols = pl.ds(lo, width)
        if a == "x":
            for x in range(4):
                src, dst = tok.at[pl.ds(32 * x, 32), cols], buf.at[co["y"], co["z"], x, :, cols]
                owns.append(pltpu.make_async_copy(src, dst, local.at[6 + len(owns)]))
        else:
            src, dst = tok.at[shard, cols], buf.at[co["y"], co["z"], co["x"], :, cols]
            owns.append(pltpu.make_async_copy(src, dst, local.at[6 + len(owns)]))
    for own in owns:
        own.start()
    c2 = pl.ds(co["c"] * 2, 2)
    moves = (
        (wg, vgu.at[c2, pl.ds(0, 352)]),
        (wu, vgu.at[c2, pl.ds(352, 352)]),
        (wd, vd.at[c2]),
        (lm, words.at[co["c"]]),
    )
    loads = [pltpu.make_async_copy(src, dst, local.at[1 + i]) for i, (src, dst) in enumerate(moves)]
    again = pltpu.make_async_copy(tok.at[shard], mine, local.at[5])
    zero = jnp.zeros((2, 128), F32)
    info[0] = jnp.concatenate([ids[...].astype(F32), zero, weight[...], targets[...].astype(F32), zero[0:1]], axis=0)
    for own in owns:
        own.wait()
    for load in loads + [again]:
        load.start()
    pl.semaphore_wait(barrier, 22)
    swaps = [remote(src, dst, wsend.at[i], wrecv.at[i], sibling) for i, (src, dst) in enumerate(moves)]

    def tell(r, _):
        remote(info.at[0], info.at[r], isend, irecv, plane_peer(co, r)).start()
        return 0

    lax.fori_loop(1, 16, tell, 0)
    for s in swaps:
        s.start()
    sc_first, sc_second, sc_third = scatter_rings(part, land_c, land_b, land_a, co, sc_send, sc_recv)

    def routes():
        others = info.at[pl.ds(1, 15)]
        pltpu.make_async_copy(others, others, irecv).wait()
        pltpu.make_async_copy(others, others, isend).wait()

        def read_source(q, _):
            got_info = info[(q_me - q + 16) % 16]
            named, by = got_info[0:6], got_info[8:14]
            mask_rows, gate_rows = [], []
            for l in range(4):
                hit = named == (4 * q_me + l).astype(F32)
                mask_rows.append(jnp.sum(jnp.where(hit, 1.0, 0.0), axis=0, keepdims=True))
                gate_rows.append(jnp.sum(jnp.where(hit, by, 0.0), axis=0, keepdims=True))
            none = jnp.zeros((4, 128), F32)
            at = pl.ds(pl.multiple_of(q * 8, 8), 8)
            masks[at] = jnp.concatenate(mask_rows + [none], axis=0)
            gates[at] = jnp.concatenate(gate_rows + [none], axis=0)
            goals[q] = jnp.transpose(jnp.broadcast_to(got_info[14:15], (128, 128)))
            return 0

        lax.fori_loop(0, 16, read_source, 0)
        before = (
            lax.broadcasted_iota(jnp.int32, (128, 128), 0) < lax.broadcasted_iota(jnp.int32, (128, 128), 1)
        ).astype(F32).astype(BF)
        taken = masks[...]
        ahead = jnp.dot(taken.astype(BF), before, preferred_element_type=F32)
        places[...] = jnp.where(taken > 0.0, ahead, -1.0)

        def picking(p, _):
            slot = lax.broadcasted_iota(jnp.int32, (24, 128), 0).astype(F32)
            none = jnp.zeros((24, 128), F32)
            at = pl.ds(pl.multiple_of(p * 16, 16), 16)
            place, by = places[at], gates[at]
            pick = []
            for l in range(4):
                for s in range(2):
                    k = s * 8 + l
                    hit = jnp.where(place[k : k + 1] == slot, 1.0, 0.0)
                    pick.append(jnp.concatenate([hit, none] if s == 0 else [none, hit], axis=1))
                    row_gate[l, pl.ds(pl.multiple_of(p * 48 + s * 24, 8), 24)] = jnp.sum(
                        hit * by[k : k + 1], axis=1, keepdims=True
                    )
            picks[p] = jnp.concatenate(pick, axis=0).astype(BF)
            return 0

        lax.fori_loop(0, 8, picking, 0)
        for i in range(3):
            loads[i].wait()
            swaps[i].wait()

    def experts(j, half_way=None):
        if j not in (LEFT, FAR):
            return
        pair = (OWN, LEFT) if j == LEFT else (RIGHT, FAR)
        ys = [shift(co, "y", GROUPS[k]) for k in pair]

        def place_of(t):
            return jnp.where(t < 2, ys[0], ys[1]), t % 2

        def select(t, _):
            y, i = place_of(t)
            two = buf[y, pl.ds(2 * i, 2)].reshape(256, 2048)
            chosen = jnp.dot(picks[2 * y + i], two, preferred_element_type=F32).astype(BF)
            for l in range(4):
                rows[l, pl.ds(pl.multiple_of(t * 48, 16), 48)] = chosen[l * 48 : (l + 1) * 48]
            return 0

        lax.fori_loop(0, 4, select, 0)

        def ffn(l, _):
            both = lax.dot_general(rows[l], vgu[l], (((1,), (1,)), ((), ())), preferred_element_type=F32)
            gate, up = both[:, 0:352], both[:, 352:704]
            hidden = (gate / (1.0 + jnp.exp(-gate)) * up).astype(BF)
            scale = jnp.concatenate([row_gate[l, pl.ds(pl.multiple_of(y * 96, 8), 96)] for y in ys], axis=0)
            rows[l] = (jnp.dot(hidden, vd[l], preferred_element_type=F32) * scale).astype(BF)
            return 0

        lax.fori_loop(0, 2, ffn, 0)
        if j == LEFT:
            half_way()
        else:
            for n in (0, 1):
                sc_first[n][OWN].forward()
                sc_first[n][LEFT].forward()
        lax.fori_loop(2, 4, ffn, 0)

        def combine(t, _):
            y, i = place_of(t)
            at = pl.ds(pl.multiple_of(t * 48, 16), 48)
            shares = jnp.concatenate([rows[l, at] for l in range(4)], axis=0)
            mixed = lax.dot_general(picks[2 * y + i], shares, (((0,), (0,)), ((), ())), preferred_element_type=F32)
            part[y, pl.ds(2 * i, 2)] = mixed.astype(BF).reshape(2, 4, 32, 2048)
            return 0

        lax.fori_loop(0, 4, combine, 0)
        for n in (0, 1):
            for k in (OWN, LEFT) if j == LEFT else (FAR, RIGHT):
                sc_first[n][k].start()

    lines = gather_groups(buf, co, ga_send.at[0], ga_recv.at[0], True, routes, experts)
    drain(buf, ga_send.at[0], COLORS, co, lines)
    for j in (FAR, LEFT, RIGHT, OWN):
        sc_first[2][j].start()
    for n in (0, 1, 2):
        sc_first[n][FAR].forward()
    sc_first[2][LEFT].forward()
    for n in (0, 1):
        sc_first[n][RIGHT].forward()
    for n in (0, 1, 2):
        sc_first[n][FAR].finish()
        sc_second[n].start()
    sc_first[2][RIGHT].forward()
    sc_first[2][OWN].forward()
    for n in (0, 1, 2):
        sc_first[n][LEFT].finish()
        sc_first[n][RIGHT].finish()
        sc_second[n].forward()
    for n in (0, 1, 2):
        sc_first[n][OWN].finish()
    for n in (0, 1, 2):
        sc_second[n].finish()
        sc_third[n].start()
    for n in (0, 1, 2):
        sc_third[n].finish()
    again.wait()
    resid = (mine[...].astype(F32) + part[co["y"], co["z"], co["x"]].astype(F32)).astype(BF).astype(F32)
    square = jnp.mean(resid * resid, axis=1, keepdims=True)
    buf[co["y"], co["z"], co["x"]] = (resid * lax.rsqrt(square + 1e-06) * gain[...]).astype(BF)

    def words_ready():
        loads[3].wait()
        swaps[3].wait()
        drain(part, sc_send, BACK, co, range(3))

    def head(j, half_way=None):
        y = shift(co, "y", GROUPS[j])

        def pair(i, _):
            lane = lax.broadcasted_iota(jnp.int32, (128, 128), 1)
            column = lax.broadcasted_iota(jnp.int32, (256, 768), 1)
            two = buf[y, pl.ds(2 * i, 2)].reshape(256, 2048)
            q = 4 * y + 2 * i
            goal = jnp.concatenate([goals[q + s][:, 0:1] for s in range(2)], axis=0).astype(jnp.int32)
            logits = [jnp.dot(two, words[v], preferred_element_type=F32) for v in range(2)]
            top = jnp.maximum(*[jnp.max(value, axis=1, keepdims=True) for value in logits])
            total, chosen = 0.0, 0.0
            for v in range(2):
                base = ((q_me * 2 + v) * 4 + co["x"]) * 768
                total += jnp.sum(jnp.exp(logits[v] - top), axis=1, keepdims=True)
                chosen += jnp.sum(jnp.where(column == goal - base, logits[v], 0.0), axis=1, keepdims=True)
            norm = top + jnp.log(total)
            for s in range(2):
                at = slice(s * 128, (s + 1) * 128)
                both = jnp.where(lane == 0, norm[at], jnp.where(lane == 1, chosen[at], 0.0))
                stats[q + s] = jnp.transpose(both)[0:2]
            return 0

        if half_way is None:
            lax.fori_loop(0, 2, pair, 0)
        else:
            lax.fori_loop(0, 1, pair, 0)
            half_way()
            lax.fori_loop(1, 2, pair, 0)

    def note(j, i):
        y, z, x = shift(co, "y", GROUPS[j]), (co["z"] + i // 4) % 4, (co["x"] + i) % 4
        slot = (GROUPS[j] % 4) * 16 + i
        return remote(stats.at[4 * y + z], got.at[slot], st_send, st_recv, device(co, y=y, z=z, x=x))

    def head_and_send(j, half_way=None):
        head(j, half_way)

        def send(i, _):
            note(j, i).start()
            return 0

        lax.fori_loop(1 if j == OWN else 0, 16, send, 0)

    lines = gather_groups(buf, co, ga_send.at[1], ga_recv.at[1], False, words_ready, head_and_send)
    got[0] = stats[q_me]
    drain(buf, ga_send.at[1], COLORS, co, lines)
    others = got.at[pl.ds(1, 63)]
    pltpu.make_async_copy(others, others, st_send).wait()
    pltpu.make_async_copy(others, others, st_recv).wait()
    norms = got[:, 0, :]
    best = jnp.max(norms, axis=0, keepdims=True)
    mass = jnp.sum(jnp.exp(norms - best), axis=0, keepdims=True)
    chosen = jnp.sum(got[:, 1, :], axis=0, keepdims=True)
    out[...] = chosen - best - jnp.log(mass)


def vmem(*shape, dtype=BF):
    return pltpu.VMEM(shape, dtype)


def body(tokens, expert_ids, gates, w_gate, w_up, w_down, norm_gain, lm_weight, targets):
    hbm, chip = pl.BlockSpec(memory_space=pl.ANY), pl.BlockSpec(memory_space=pltpu.VMEM)
    dma = pltpu.SemaphoreType.DMA
    out = pl.pallas_call(
        kernel,
        out_shape=jax.ShapeDtypeStruct((1, 128), F32),
        in_specs=[hbm, chip, chip, chip, hbm, hbm, hbm, chip, hbm],
        out_specs=chip,
        scratch_shapes=[
            vmem(4, 4, 4, 32, 2048), vmem(4, 704, 2048), vmem(4, 352, 2048), vmem(16, 16, 128, dtype=F32),
            vmem(4, 4, 4, 32, 2048), vmem(4, 3, 4, 32, 2048), vmem(3, 4, 32, 2048), vmem(3, 32, 2048),
            vmem(2, 2048, 768), vmem(32, 2048), vmem(16, 128, 128, dtype=F32),
            vmem(16, 2, 128, dtype=F32), vmem(64, 2, 128, dtype=F32),
            vmem(4, 192, 2048), vmem(8, 192, 256), vmem(4, 384, 1, dtype=F32),
            vmem(128, 128, dtype=F32), vmem(128, 128, dtype=F32), vmem(128, 128, dtype=F32),
            dma((2, 3, 3)), dma((2, 3, 6, 3)), dma((3, 3)), dma((3, 6, 3)), dma, dma,
            dma, dma, dma((4,)), dma((4,)), dma((15,)),
        ],
        compiler_params=pltpu.CompilerParams(collective_id=0, has_side_effects=True, vmem_limit_bytes=67043328),
        name="layer",
    )(
        tokens, expert_ids.T, gates.T, targets[None], jnp.swapaxes(w_gate, 1, 2), jnp.swapaxes(w_up, 1, 2), w_down,
        norm_gain[None], lm_weight,
    )
    return out[0]


def solution(mesh):
    in_specs = (
        P("expert", None),
        P("expert", None),
        P("expert", None),
        P("expert", None, "vocab"),
        P("expert", None, "vocab"),
        P("expert", "vocab", None),
        P(),
        P(None, ("expert", "vocab")),
        P("expert"),
    )
    return jax.shard_map(body, mesh=mesh, in_specs=in_specs, out_specs=P("expert"), check_vma=False)
```

```python
import jax
import jax.numpy as jnp
from jax import lax
from jax.experimental import pallas as pl
from jax.experimental.pallas import tpu as pltpu
from jax.sharding import PartitionSpec as P

MESH = pl.DeviceIdType.MESH
BF = jnp.bfloat16
F32 = jnp.float32
COLORS = (("x", "y", "z", 0, 768), ("z", "y", "x", 768, 768), ("x", "z", "y", 1536, 512))
BACK = (("x", "y", "z", 0, 768), ("z", "y", "x", 768, 896), ("x", "z", "y", 1664, 384))
GROUPS = (0, -1, 1, 2)
OWN, LEFT, RIGHT, FAR = range(4)


def coords():
    e = lax.axis_index("expert")
    return {"x": lax.axis_index("vocab"), "y": e // 8, "z": (e // 2) % 4, "c": e % 2}


def device(co, **changed):
    q = dict(co, **changed)
    return {"expert": (q["y"] * 4 + q["z"]) * 2 + q["c"], "vocab": q["x"]}


def shift(co, dim, by):
    return (co[dim] + by) % 4


def view(buf, idx, cols, half=None):
    rows = slice(None) if half is None else pl.ds(16 * half, 16)
    y, z, x = (pl.ds(0, 4) if idx[d] is None else idx[d] for d in "yzx")
    return buf.at[y, z, x, rows, pl.ds(cols[0], cols[1])]


def remote(src, dst, ssem, rsem, to):
    return pltpu.make_async_remote_copy(src, dst, ssem, rsem, device_id=to, device_id_type=MESH)


class GatherRing:
    def __init__(self, buf, co, dim, idx, cols, ssem, rsem):
        self.buf, self.co, self.dim, self.idx, self.cols = buf, co, dim, idx, cols
        self.ssem, self.rsem = ssem, rsem
        self.left, self.right = shift(co, dim, -1), shift(co, dim, 1)
        self.far, self.me = shift(co, dim, 2), co[dim]

    def copy(self, n, k, half, to):
        ref = view(self.buf, dict(self.idx, **{self.dim: k}), self.cols, half)
        return remote(ref, ref, self.ssem, self.rsem.at[n], device(self.co, **{self.dim: to}))

    def start(self):
        self.copy(0, self.me, None, self.right).start()
        self.copy(1, self.me, None, self.left).start()

    def forward(self):
        self.copy(0, self.left, None, self.right).wait_recv()
        self.copy(2, self.left, 0, self.right).start()
        self.copy(1, self.right, None, self.left).wait_recv()
        self.copy(2, self.right, 1, self.left).start()

    def finish(self):
        self.copy(2, self.far, None, self.right).wait_recv()


class GatherLine(GatherRing):
    def start(self):
        for n, to in enumerate((self.right, self.left, self.far)):
            self.copy(n, self.me, None, to).start()

    def finish(self):
        for n, k in enumerate((self.left, self.right, self.far)):
            self.copy(n, k, None, self.far).wait_recv()


def drain(buf, sems, colors, co, lines):
    for n, (_, _, _, lo, width) in enumerate(colors):
        cols = pl.ds(lo, width)
        sizes = (buf.at[0, 0, pl.ds(0, 3), :, cols], buf.at[pl.ds(0, 3), :, 0, :, cols], buf.at[pl.ds(0, 3), :, :, :, cols])
        for kind in range(3):
            if kind or n in lines:
                pltpu.make_async_copy(sizes[kind], sizes[kind], sems.at[n, kind]).wait()


def gather_groups(buf, co, ssem, rsem, have_x, idle, group):
    first, second, third = [], [], []
    for n, (a, b, c, lo, width) in enumerate(COLORS):
        base = {d: co[d] for d in "xyz"}
        first.append(GatherLine(buf, co, a, base, (lo, width), ssem.at[n, 0], rsem.at[n, 0]))
        line = dict(base, **{a: None})
        second.append(GatherRing(buf, co, b, line, (lo, width), ssem.at[n, 1], rsem.at[n, 1]))
        third.append(
            [
                GatherRing(buf, co, c, dict(line, **{b: shift(co, b, k)}), (lo, width), ssem.at[n, 2], rsem.at[n, 2 + j])
                for j, k in enumerate(GROUPS)
            ]
        )
    needed = [n for n in range(3) if not (have_x and COLORS[n][0] == "x")]
    ready = [n for n in range(3) if n not in needed]
    for n in needed:
        first[n].start()
    for n in ready:
        second[n].start()
    for n in ready:
        if n < 2:
            third[n][OWN].start()
    for n in needed:
        first[n].finish()
        second[n].start()
        if n < 2:
            third[n][OWN].start()
    second[0].forward()
    third[0][LEFT].start()
    third[1][OWN].forward()
    third[0][OWN].forward()
    second[2].forward()
    second[1].forward()
    third[1][LEFT].start()
    third[1][RIGHT].start()
    for j in (OWN, LEFT, RIGHT):
        third[2][j].start()
    third[0][LEFT].forward()
    third[0][RIGHT].start()
    second[0].finish()
    third[0][FAR].start()
    second[1].finish()
    second[2].finish()
    third[2][FAR].start()
    idle()
    for n in (0, 1):
        third[n][OWN].finish()

    def left_on():
        third[1][LEFT].forward()
        third[1][FAR].start()
        third[2][OWN].forward()

    group(OWN, left_on)
    third[2][LEFT].forward()
    for n in (1, 0):
        third[n][RIGHT].forward()
    third[2][RIGHT].forward()
    for n in (0, 1):
        third[n][LEFT].finish()
    third[2][FAR].forward()

    def far_on():
        for n in (0, 1):
            third[n][FAR].forward()

    group(LEFT, far_on)
    for n in (0, 1):
        third[n][RIGHT].finish()
    group(RIGHT)
    for n in (0, 1):
        third[n][FAR].finish()
    for j in range(4):
        third[2][j].finish()
    group(FAR)
    return needed


class ScatterRing:
    def __init__(self, acc, land, co, dim, idx, cols, ssem, rsem):
        self.acc, self.co, self.dim, self.idx, self.cols = acc, co, dim, idx, cols
        self.land, self.ssem, self.rsem = land, ssem, rsem
        self.left, self.right = shift(co, dim, -1), shift(co, dim, 1)
        self.far, self.me = shift(co, dim, 2), co[dim]

    def piece(self, k, half=None):
        return view(self.acc, dict(self.idx, **{self.dim: k}), self.cols, half)

    def landing(self, n):
        cols = pl.ds(self.cols[0], self.cols[1])
        full = [slice(None)] * (len(self.land.shape) - 3)
        if n < 2:
            return self.land.at[(0, *full, pl.ds(16 * n, 16), cols)]
        return self.land.at[(n - 1, *full, slice(None), cols)]

    def copy(self, n, src, to):
        sem = self.rsem.at[min(n, 2)]
        return remote(src, self.landing(n), self.ssem, sem, device(self.co, **{self.dim: to}))

    def add(self, k, half, *numbers):
        at, parts = self.piece(k, half), [self.landing(n) for n in numbers]
        if len(at.shape) == 2:
            total = at[...].astype(F32)
            for got in parts:
                total = total + got[...].astype(F32)
            at[...] = total.astype(BF)
        else:

            def one(i, _):
                total = at[i].astype(F32)
                for got in parts:
                    total = total + got[i].astype(F32)
                at[i] = total.astype(BF)
                return 0

            lax.fori_loop(0, at.shape[0], one, 0)

    def start(self):
        self.copy(0, self.piece(self.far, 0), self.left).start()
        self.copy(1, self.piece(self.far, 1), self.right).start()

    def forward(self):
        self.copy(0, self.piece(self.left, 0), self.left).wait_recv()
        self.add(self.left, 0, 0)
        self.copy(2, self.piece(self.left), self.left).start()
        self.copy(1, self.piece(self.right, 1), self.right).wait_recv()
        self.add(self.right, 1, 1)
        self.copy(3, self.piece(self.right), self.right).start()

    def finish(self):
        cols = pl.ds(self.cols[0], self.cols[1])
        full = [slice(None)] * (len(self.land.shape) - 2)
        both = self.land.at[(pl.ds(1, 2), *full, cols)]
        pltpu.make_async_copy(both, both, self.rsem.at[2]).wait()
        self.add(self.me, None, 2, 3)


class ScatterLine(ScatterRing):
    def copy(self, n, src, to):
        land = self.land.at[n, :, pl.ds(self.cols[0], self.cols[1])]
        return remote(src, land, self.ssem, self.rsem.at[n], device(self.co, **{self.dim: to}))

    def landing(self, n):
        return self.land.at[n, :, pl.ds(self.cols[0], self.cols[1])]

    def start(self):
        for n, to in enumerate((self.right, self.left, self.far)):
            self.copy(n, self.piece(to), to).start()

    def finish(self):
        for n in range(3):
            self.copy(n, self.piece(self.me), self.far).wait_recv()
        self.add(self.me, None, 0, 1, 2)


def scatter_rings(acc, land_c, land_b, land_a, co, ssem, rsem):
    first, second, third = [], [], []
    for n, (a, b, c, lo, width) in enumerate(BACK):
        base = {d: co[d] for d in "xyz"}
        cols = (lo, width)
        line = dict(base, **{a: None})
        first.append(
            [
                ScatterRing(acc, land_c.at[j], co, c, dict(line, **{b: shift(co, b, k)}), cols, ssem.at[n, 2], rsem.at[n, 2 + j])
                for j, k in enumerate(GROUPS)
            ]
        )
        second.append(ScatterRing(acc, land_b, co, b, line, cols, ssem.at[n, 1], rsem.at[n, 1]))
        third.append(ScatterLine(acc, land_a, co, a, base, cols, ssem.at[n, 0], rsem.at[n, 0]))
    return first, second, third


def greet(barrier, to):
    pl.semaphore_signal(barrier, inc=1, device_id=to, device_id_type=MESH)


def greet_neighbours(co, barrier):
    for dim in "xyz":
        for by in (1, -1):
            greet(barrier, device(co, **{dim: shift(co, dim, by)}))
    greet(barrier, device(co, c=1 - co["c"]))


def plane_peer(co, r):
    q = (co["y"] * 4 + co["z"] + r) % 16
    return device(co, y=q // 4, z=q % 4)


def kernel(
    tok, ids, weight, targets, wg, wu, wd, gain, lm, out,
    buf, vgu, vd, info, part, land_c, land_b, land_a, words, mine, goals, stats, got,
    rows, picks, row_gate, masks, gates, places,
    ga_send, ga_recv, sc_send, sc_recv, st_send, st_recv, isend, irecv, wsend, wrecv, local,
):
    co = coords()
    q_me = co["y"] * 4 + co["z"]
    sibling = device(co, c=1 - co["c"])
    barrier = pltpu.get_barrier_semaphore()
    greet_neighbours(co, barrier)

    def greet_peer(r, _):
        greet(barrier, plane_peer(co, r))
        return 0

    lax.fori_loop(1, 16, greet_peer, 0)
    shard = pl.ds(pl.multiple_of(co["x"] * 32, 32), 32)
    owns = []
    for n, (a, _, _, lo, width) in enumerate(COLORS):
        cols = pl.ds(lo, width)
        if a == "x":
            for x in range(4):
                src, dst = tok.at[pl.ds(32 * x, 32), cols], buf.at[co["y"], co["z"], x, :, cols]
                owns.append(pltpu.make_async_copy(src, dst, local.at[6 + len(owns)]))
        else:
            src, dst = tok.at[shard, cols], buf.at[co["y"], co["z"], co["x"], :, cols]
            owns.append(pltpu.make_async_copy(src, dst, local.at[6 + len(owns)]))
    for own in owns:
        own.start()
    c2 = pl.ds(co["c"] * 2, 2)
    moves = (
        (wg, vgu.at[c2, pl.ds(0, 352)]),
        (wu, vgu.at[c2, pl.ds(352, 352)]),
        (wd, vd.at[c2]),
        (lm, words.at[co["c"]]),
    )
    loads = [pltpu.make_async_copy(src, dst, local.at[1 + i]) for i, (src, dst) in enumerate(moves)]
    again = pltpu.make_async_copy(tok.at[shard], mine, local.at[5])
    zero = jnp.zeros((2, 128), F32)
    info[0] = jnp.concatenate([ids[...].astype(F32), zero, weight[...], targets[...].astype(F32), zero[0:1]], axis=0)
    for own in owns:
        own.wait()
    for load in loads + [again]:
        load.start()
    pl.semaphore_wait(barrier, 22)
    swaps = [remote(src, dst, wsend.at[i], wrecv.at[i], sibling) for i, (src, dst) in enumerate(moves)]

    def tell(r, _):
        remote(info.at[0], info.at[r], isend, irecv, plane_peer(co, r)).start()
        return 0

    lax.fori_loop(1, 16, tell, 0)
    for s in swaps:
        s.start()
    sc_first, sc_second, sc_third = scatter_rings(part, land_c, land_b, land_a, co, sc_send, sc_recv)

    def routes():
        others = info.at[pl.ds(1, 15)]
        pltpu.make_async_copy(others, others, irecv).wait()
        pltpu.make_async_copy(others, others, isend).wait()

        def read_source(q, _):
            got_info = info[(q_me - q + 16) % 16]
            named, by = got_info[0:6], got_info[8:14]
            mask_rows, gate_rows = [], []
            for l in range(4):
                hit = named == (4 * q_me + l).astype(F32)
                mask_rows.append(jnp.sum(jnp.where(hit, 1.0, 0.0), axis=0, keepdims=True))
                gate_rows.append(jnp.sum(jnp.where(hit, by, 0.0), axis=0, keepdims=True))
            none = jnp.zeros((4, 128), F32)
            at = pl.ds(pl.multiple_of(q * 8, 8), 8)
            masks[at] = jnp.concatenate(mask_rows + [none], axis=0)
            gates[at] = jnp.concatenate(gate_rows + [none], axis=0)
            goals[q] = jnp.transpose(jnp.broadcast_to(got_info[14:15], (128, 128)))
            return 0

        lax.fori_loop(0, 16, read_source, 0)
        before = (
            lax.broadcasted_iota(jnp.int32, (128, 128), 0) < lax.broadcasted_iota(jnp.int32, (128, 128), 1)
        ).astype(F32).astype(BF)
        taken = masks[...]
        ahead = jnp.dot(taken.astype(BF), before, preferred_element_type=F32)
        places[...] = jnp.where(taken > 0.0, ahead, -1.0)

        def picking(p, _):
            slot = lax.broadcasted_iota(jnp.int32, (24, 128), 0).astype(F32)
            none = jnp.zeros((24, 128), F32)
            at = pl.ds(pl.multiple_of(p * 16, 16), 16)
            place, by = places[at], gates[at]
            pick = []
            for l in range(4):
                for s in range(2):
                    k = s * 8 + l
                    hit = jnp.where(place[k : k + 1] == slot, 1.0, 0.0)
                    pick.append(jnp.concatenate([hit, none] if s == 0 else [none, hit], axis=1))
                    row_gate[l, pl.ds(pl.multiple_of(p * 48 + s * 24, 8), 24)] = jnp.sum(
                        hit * by[k : k + 1], axis=1, keepdims=True
                    )
            picks[p] = jnp.concatenate(pick, axis=0).astype(BF)
            return 0

        lax.fori_loop(0, 8, picking, 0)
        for i in range(3):
            loads[i].wait()
            swaps[i].wait()

    def experts(j, half_way=None):
        if j not in (LEFT, FAR):
            if half_way:
                half_way()
            return
        pair = (OWN, LEFT) if j == LEFT else (RIGHT, FAR)
        ys = [shift(co, "y", GROUPS[k]) for k in pair]

        def place_of(t):
            return jnp.where(t < 2, ys[0], ys[1]), t % 2

        def select(t, _):
            y, i = place_of(t)
            two = buf[y, pl.ds(2 * i, 2)].reshape(256, 2048)
            chosen = jnp.dot(picks[2 * y + i], two, preferred_element_type=F32).astype(BF)
            for l in range(4):
                rows[l, pl.ds(pl.multiple_of(t * 48, 16), 48)] = chosen[l * 48 : (l + 1) * 48]
            return 0

        lax.fori_loop(0, 4, select, 0)

        def ffn(l, _):
            @pl.when(l == 2)
            def _():
                if j == LEFT:
                    half_way()
                else:
                    for n in (0, 1):
                        sc_first[n][OWN].forward()
                        sc_first[n][LEFT].forward()

            both = lax.dot_general(rows[l], vgu[l], (((1,), (1,)), ((), ())), preferred_element_type=F32)
            gate, up = both[:, 0:352], both[:, 352:704]
            hidden = (gate / (1.0 + jnp.exp(-gate)) * up).astype(BF)
            scale = jnp.concatenate([row_gate[l, pl.ds(pl.multiple_of(y * 96, 8), 96)] for y in ys], axis=0)
            rows[l] = (jnp.dot(hidden, vd[l], preferred_element_type=F32) * scale).astype(BF)
            return 0

        lax.fori_loop(0, 4, ffn, 0)

        def combine(t, _):
            y, i = place_of(t)
            at = pl.ds(pl.multiple_of(t * 48, 16), 48)
            shares = jnp.concatenate([rows[l, at] for l in range(4)], axis=0)
            mixed = lax.dot_general(picks[2 * y + i], shares, (((0,), (0,)), ((), ())), preferred_element_type=F32)
            part[y, pl.ds(2 * i, 2)] = mixed.astype(BF).reshape(2, 4, 32, 2048)
            return 0

        lax.fori_loop(0, 4, combine, 0)
        for n in (0, 1):
            for k in (OWN, LEFT) if j == LEFT else (FAR, RIGHT):
                sc_first[n][k].start()

    lines = gather_groups(buf, co, ga_send.at[0], ga_recv.at[0], True, routes, experts)
    drain(buf, ga_send.at[0], COLORS, co, lines)
    for j in (FAR, LEFT, RIGHT, OWN):
        sc_first[2][j].start()
    for n in (0, 1, 2):
        sc_first[n][FAR].forward()
    sc_first[2][LEFT].forward()
    for n in (0, 1):
        sc_first[n][RIGHT].forward()
    for n in (0, 1, 2):
        sc_first[n][FAR].finish()
        sc_second[n].start()
    sc_first[2][RIGHT].forward()
    sc_first[2][OWN].forward()
    for n in (0, 1, 2):
        sc_first[n][LEFT].finish()
        sc_first[n][RIGHT].finish()
        sc_second[n].forward()
    for n in (0, 1, 2):
        sc_first[n][OWN].finish()
    for n in (0, 1, 2):
        sc_second[n].finish()
        sc_third[n].start()
    for n in (0, 1, 2):
        sc_third[n].finish()
    again.wait()
    resid = (mine[...].astype(F32) + part[co["y"], co["z"], co["x"]].astype(F32)).astype(BF).astype(F32)
    square = jnp.mean(resid * resid, axis=1, keepdims=True)
    buf[co["y"], co["z"], co["x"]] = (resid * lax.rsqrt(square + 1e-06) * gain[...]).astype(BF)

    def words_ready():
        loads[3].wait()
        swaps[3].wait()
        drain(part, sc_send, BACK, co, range(3))

    def head(j, half_way=None):
        y = shift(co, "y", GROUPS[j])

        def pair(i, _):
            if half_way:
                pl.when(i == 1)(half_way)

            lane = lax.broadcasted_iota(jnp.int32, (128, 128), 1)
            column = lax.broadcasted_iota(jnp.int32, (256, 768), 1)
            two = buf[y, pl.ds(2 * i, 2)].reshape(256, 2048)
            q = 4 * y + 2 * i
            goal = jnp.concatenate([goals[q + s][:, 0:1] for s in range(2)], axis=0).astype(jnp.int32)
            logits = [jnp.dot(two, words[v], preferred_element_type=F32) for v in range(2)]
            top = jnp.maximum(*[jnp.max(value, axis=1, keepdims=True) for value in logits])
            total, chosen = 0.0, 0.0
            for v in range(2):
                base = ((q_me * 2 + v) * 4 + co["x"]) * 768
                total += jnp.sum(jnp.exp(logits[v] - top), axis=1, keepdims=True)
                chosen += jnp.sum(jnp.where(column == goal - base, logits[v], 0.0), axis=1, keepdims=True)
            norm = top + jnp.log(total)
            for s in range(2):
                at = slice(s * 128, (s + 1) * 128)
                both = jnp.where(lane == 0, norm[at], jnp.where(lane == 1, chosen[at], 0.0))
                stats[q + s] = jnp.transpose(both)[0:2]
            return 0

        lax.fori_loop(0, 2, pair, 0)

    def note(j, i):
        y, z, x = shift(co, "y", GROUPS[j]), (co["z"] + i // 4) % 4, (co["x"] + i) % 4
        slot = (GROUPS[j] % 4) * 16 + i
        return remote(stats.at[4 * y + z], got.at[slot], st_send, st_recv, device(co, y=y, z=z, x=x))

    def head_and_send(j, half_way=None):
        head(j, half_way)

        def send(i, _):
            note(j, i).start()
            return 0

        lax.fori_loop(1 if j == OWN else 0, 16, send, 0)

    lines = gather_groups(buf, co, ga_send.at[1], ga_recv.at[1], False, words_ready, head_and_send)
    got[0] = stats[q_me]
    drain(buf, ga_send.at[1], COLORS, co, lines)
    others = got.at[pl.ds(1, 63)]
    pltpu.make_async_copy(others, others, st_send).wait()
    pltpu.make_async_copy(others, others, st_recv).wait()
    norms = got[:, 0, :]
    best = jnp.max(norms, axis=0, keepdims=True)
    mass = jnp.sum(jnp.exp(norms - best), axis=0, keepdims=True)
    chosen = jnp.sum(got[:, 1, :], axis=0, keepdims=True)
    out[...] = chosen - best - jnp.log(mass)


def vmem(*shape, dtype=BF):
    return pltpu.VMEM(shape, dtype)


def body(tokens, expert_ids, gates, w_gate, w_up, w_down, norm_gain, lm_weight, targets):
    hbm, chip = pl.BlockSpec(memory_space=pl.ANY), pl.BlockSpec(memory_space=pltpu.VMEM)
    dma = pltpu.SemaphoreType.DMA
    out = pl.pallas_call(
        kernel,
        out_shape=jax.ShapeDtypeStruct((1, 128), F32),
        in_specs=[hbm, chip, chip, chip, hbm, hbm, hbm, chip, hbm],
        out_specs=chip,
        scratch_shapes=[
            vmem(4, 4, 4, 32, 2048), vmem(4, 704, 2048), vmem(4, 352, 2048), vmem(16, 16, 128, dtype=F32),
            vmem(4, 4, 4, 32, 2048), vmem(4, 3, 4, 32, 2048), vmem(3, 4, 32, 2048), vmem(3, 32, 2048),
            vmem(2, 2048, 768), vmem(32, 2048), vmem(16, 128, 128, dtype=F32),
            vmem(16, 2, 128, dtype=F32), vmem(64, 2, 128, dtype=F32),
            vmem(4, 192, 2048), vmem(8, 192, 256), vmem(4, 384, 1, dtype=F32),
            vmem(128, 128, dtype=F32), vmem(128, 128, dtype=F32), vmem(128, 128, dtype=F32),
            dma((2, 3, 3)), dma((2, 3, 6, 3)), dma((3, 3)), dma((3, 6, 3)), dma, dma,
            dma, dma, dma((4,)), dma((4,)), dma((15,)),
        ],
        compiler_params=pltpu.CompilerParams(collective_id=0, has_side_effects=True, vmem_limit_bytes=67043328),
        name="layer",
    )(
        tokens, expert_ids.T, gates.T, targets[None], jnp.swapaxes(w_gate, 1, 2), jnp.swapaxes(w_up, 1, 2), w_down,
        norm_gain[None], lm_weight,
    )
    return out[0]


def solution(mesh):
    in_specs = (
        P("expert", None),
        P("expert", None),
        P("expert", None),
        P("expert", None, "vocab"),
        P("expert", None, "vocab"),
        P("expert", "vocab", None),
        P(),
        P(None, ("expert", "vocab")),
        P("expert"),
    )
    return jax.shard_map(body, mesh=mesh, in_specs=in_specs, out_specs=P("expert"), check_vma=False)
```

```python
import jax
import jax.numpy as jnp
from jax import lax
from jax.experimental import pallas as pl
from jax.experimental.pallas import tpu as pltpu
from jax.sharding import PartitionSpec as P

MESH = pl.DeviceIdType.MESH
BF = jnp.bfloat16
F32 = jnp.float32
COLORS = (("x", "y", "z", 0, 768), ("z", "y", "x", 768, 768), ("x", "z", "y", 1536, 512))
BACK = (("x", "y", "z", 0, 768), ("z", "y", "x", 768, 896), ("x", "z", "y", 1664, 384))
GROUPS = (0, -1, 1, 2)
OWN, LEFT, RIGHT, FAR = range(4)


def coords():
    e = lax.axis_index("expert")
    return {"x": lax.axis_index("vocab"), "y": e // 8, "z": (e // 2) % 4, "c": e % 2}


def device(co, **changed):
    q = dict(co, **changed)
    return {"expert": (q["y"] * 4 + q["z"]) * 2 + q["c"], "vocab": q["x"]}


def shift(co, dim, by):
    return (co[dim] + by) % 4


def view(buf, idx, cols, half=None):
    rows = slice(None) if half is None else pl.ds(16 * half, 16)
    y, z, x = (pl.ds(0, 4) if idx[d] is None else idx[d] for d in "yzx")
    return buf.at[y, z, x, rows, pl.ds(cols[0], cols[1])]


def remote(src, dst, ssem, rsem, to):
    return pltpu.make_async_remote_copy(src, dst, ssem, rsem, device_id=to, device_id_type=MESH)


class GatherRing:
    def __init__(self, buf, co, dim, idx, cols, ssem, rsem):
        self.buf, self.co, self.dim, self.idx, self.cols = buf, co, dim, idx, cols
        self.ssem, self.rsem = ssem, rsem
        self.left, self.right = shift(co, dim, -1), shift(co, dim, 1)
        self.far, self.me = shift(co, dim, 2), co[dim]

    def copy(self, n, k, half, to):
        ref = view(self.buf, dict(self.idx, **{self.dim: k}), self.cols, half)
        return remote(ref, ref, self.ssem, self.rsem.at[n], device(self.co, **{self.dim: to}))

    def start(self):
        self.copy(0, self.me, None, self.right).start()
        self.copy(1, self.me, None, self.left).start()

    def forward(self):
        self.copy(0, self.left, None, self.right).wait_recv()
        self.copy(2, self.left, 0, self.right).start()
        self.copy(1, self.right, None, self.left).wait_recv()
        self.copy(2, self.right, 1, self.left).start()

    def finish(self):
        self.copy(2, self.far, None, self.right).wait_recv()


class GatherLine(GatherRing):
    def start(self):
        for n, to in enumerate((self.right, self.left, self.far)):
            self.copy(n, self.me, None, to).start()

    def finish(self):
        for n, k in enumerate((self.left, self.right, self.far)):
            self.copy(n, k, None, self.far).wait_recv()


def drain(buf, sems, colors, co, lines):
    for n, (_, _, _, lo, width) in enumerate(colors):
        cols = pl.ds(lo, width)
        sizes = (buf.at[0, 0, pl.ds(0, 3), :, cols], buf.at[pl.ds(0, 3), :, 0, :, cols], buf.at[pl.ds(0, 3), :, :, :, cols])
        for kind in range(3):
            if kind or n in lines:
                pltpu.make_async_copy(sizes[kind], sizes[kind], sems.at[n, kind]).wait()


def gather_groups(buf, co, ssem, rsem, have_x, idle, group):
    first, second, third = [], [], []
    for n, (a, b, c, lo, width) in enumerate(COLORS):
        base = {d: co[d] for d in "xyz"}
        first.append(GatherLine(buf, co, a, base, (lo, width), ssem.at[n, 0], rsem.at[n, 0]))
        line = dict(base, **{a: None})
        second.append(GatherRing(buf, co, b, line, (lo, width), ssem.at[n, 1], rsem.at[n, 1]))
        third.append(
            [
                GatherRing(buf, co, c, dict(line, **{b: shift(co, b, k)}), (lo, width), ssem.at[n, 2], rsem.at[n, 2 + j])
                for j, k in enumerate(GROUPS)
            ]
        )
    needed = [n for n in range(3) if not (have_x and COLORS[n][0] == "x")]
    ready = [n for n in range(3) if n not in needed]
    for n in needed:
        first[n].start()
    for n in ready:
        second[n].start()
    for n in ready:
        if n < 2:
            third[n][OWN].start()
    for n in needed:
        first[n].finish()
        second[n].start()
        if n < 2:
            third[n][OWN].start()
    second[0].forward()
    third[0][LEFT].start()
    third[1][OWN].forward()
    third[0][OWN].forward()
    second[2].forward()
    second[1].forward()
    third[1][LEFT].start()
    third[1][RIGHT].start()
    for j in (OWN, LEFT, RIGHT):
        third[2][j].start()
    third[0][LEFT].forward()
    third[0][RIGHT].start()
    second[0].finish()
    third[0][FAR].start()
    second[1].finish()
    second[2].finish()
    third[2][FAR].start()
    idle()
    for n in (0, 1):
        third[n][OWN].finish()

    def left_on():
        third[1][LEFT].forward()
        third[1][FAR].start()
        third[2][OWN].forward()

    group(OWN, left_on)
    third[2][LEFT].forward()
    for n in (1, 0):
        third[n][RIGHT].forward()
    third[2][RIGHT].forward()
    for n in (0, 1):
        third[n][LEFT].finish()
    third[2][FAR].forward()

    def far_on():
        for n in (0, 1):
            third[n][FAR].forward()

    group(LEFT, far_on)
    for n in (0, 1):
        third[n][RIGHT].finish()
    group(RIGHT)
    for n in (0, 1):
        third[n][FAR].finish()
    for j in range(4):
        third[2][j].finish()
    group(FAR)
    return needed


class ScatterRing:
    def __init__(self, acc, land, co, dim, idx, cols, ssem, rsem):
        self.acc, self.co, self.dim, self.idx, self.cols = acc, co, dim, idx, cols
        self.land, self.ssem, self.rsem = land, ssem, rsem
        self.left, self.right = shift(co, dim, -1), shift(co, dim, 1)
        self.far, self.me = shift(co, dim, 2), co[dim]

    def piece(self, k, half=None):
        return view(self.acc, dict(self.idx, **{self.dim: k}), self.cols, half)

    def landing(self, n):
        cols = pl.ds(self.cols[0], self.cols[1])
        full = [slice(None)] * (len(self.land.shape) - 3)
        if n < 2:
            return self.land.at[(0, *full, pl.ds(16 * n, 16), cols)]
        return self.land.at[(n - 1, *full, slice(None), cols)]

    def copy(self, n, src, to):
        sem = self.rsem.at[min(n, 2)]
        return remote(src, self.landing(n), self.ssem, sem, device(self.co, **{self.dim: to}))

    def add(self, k, half, *numbers):
        at, parts = self.piece(k, half), [self.landing(n) for n in numbers]
        if len(at.shape) == 2:
            total = at[...].astype(F32)
            for got in parts:
                total = total + got[...].astype(F32)
            at[...] = total.astype(BF)
        else:

            def one(i, _):
                total = at[i].astype(F32)
                for got in parts:
                    total = total + got[i].astype(F32)
                at[i] = total.astype(BF)
                return 0

            lax.fori_loop(0, at.shape[0], one, 0)

    def start(self):
        self.copy(0, self.piece(self.far, 0), self.left).start()
        self.copy(1, self.piece(self.far, 1), self.right).start()

    def forward(self):
        self.copy(0, self.piece(self.left, 0), self.left).wait_recv()
        self.add(self.left, 0, 0)
        self.copy(2, self.piece(self.left), self.left).start()
        self.copy(1, self.piece(self.right, 1), self.right).wait_recv()
        self.add(self.right, 1, 1)
        self.copy(3, self.piece(self.right), self.right).start()

    def finish(self):
        cols = pl.ds(self.cols[0], self.cols[1])
        full = [slice(None)] * (len(self.land.shape) - 2)
        both = self.land.at[(pl.ds(1, 2), *full, cols)]
        pltpu.make_async_copy(both, both, self.rsem.at[2]).wait()
        self.add(self.me, None, 2, 3)


class ScatterLine(ScatterRing):
    def copy(self, n, src, to):
        land = self.land.at[n, :, pl.ds(self.cols[0], self.cols[1])]
        return remote(src, land, self.ssem, self.rsem.at[n], device(self.co, **{self.dim: to}))

    def landing(self, n):
        return self.land.at[n, :, pl.ds(self.cols[0], self.cols[1])]

    def start(self):
        for n, to in enumerate((self.right, self.left, self.far)):
            self.copy(n, self.piece(to), to).start()

    def finish(self):
        for n in range(3):
            self.copy(n, self.piece(self.me), self.far).wait_recv()
        self.add(self.me, None, 0, 1, 2)


def scatter_rings(acc, land_c, land_b, land_a, co, ssem, rsem):
    first, second, third = [], [], []
    for n, (a, b, c, lo, width) in enumerate(BACK):
        base = {d: co[d] for d in "xyz"}
        cols = (lo, width)
        line = dict(base, **{a: None})
        first.append(
            [
                ScatterRing(acc, land_c.at[j], co, c, dict(line, **{b: shift(co, b, k)}), cols, ssem.at[n, 2], rsem.at[n, 2 + j])
                for j, k in enumerate(GROUPS)
            ]
        )
        second.append(ScatterRing(acc, land_b, co, b, line, cols, ssem.at[n, 1], rsem.at[n, 1]))
        third.append(ScatterLine(acc, land_a, co, a, base, cols, ssem.at[n, 0], rsem.at[n, 0]))
    return first, second, third


def greet(barrier, to):
    pl.semaphore_signal(barrier, inc=1, device_id=to, device_id_type=MESH)


def greet_neighbours(co, barrier):
    for dim in "xyz":
        for by in (1, -1):
            greet(barrier, device(co, **{dim: shift(co, dim, by)}))
    greet(barrier, device(co, c=1 - co["c"]))


def plane_peer(co, r):
    q = (co["y"] * 4 + co["z"] + r) % 16
    return device(co, y=q // 4, z=q % 4)


def kernel(
    tok, ids, weight, targets, wg, wu, wd, gain, lm, out,
    buf, vgu, vd, info, part, land_c, land_b, land_a, words, mine, goals, stats, got,
    rows, picks, row_gate, masks, gates, places,
    ga_send, ga_recv, sc_send, sc_recv, st_send, st_recv, isend, irecv, wsend, wrecv, local,
):
    co = coords()
    q_me = co["y"] * 4 + co["z"]
    sibling = device(co, c=1 - co["c"])
    barrier = pltpu.get_barrier_semaphore()
    greet_neighbours(co, barrier)

    def greet_peer(r, _):
        greet(barrier, plane_peer(co, r))
        return 0

    lax.fori_loop(1, 16, greet_peer, 0)
    shard = pl.ds(pl.multiple_of(co["x"] * 32, 32), 32)
    owns = []
    for n, (a, _, _, lo, width) in enumerate(COLORS):
        cols = pl.ds(lo, width)
        if a == "x":
            for x in range(4):
                src, dst = tok.at[pl.ds(32 * x, 32), cols], buf.at[co["y"], co["z"], x, :, cols]
                owns.append(pltpu.make_async_copy(src, dst, local.at[6 + len(owns)]))
        else:
            src, dst = tok.at[shard, cols], buf.at[co["y"], co["z"], co["x"], :, cols]
            owns.append(pltpu.make_async_copy(src, dst, local.at[6 + len(owns)]))
    for own in owns:
        own.start()
    c2 = pl.ds(co["c"] * 2, 2)
    moves = (
        (wg, vgu.at[c2, pl.ds(0, 352)]),
        (wu, vgu.at[c2, pl.ds(352, 352)]),
        (wd, vd.at[c2]),
        (lm, words.at[co["c"]]),
    )
    loads = [pltpu.make_async_copy(src, dst, local.at[1 + i]) for i, (src, dst) in enumerate(moves)]
    again = pltpu.make_async_copy(tok.at[shard], mine, local.at[5])
    zero = jnp.zeros((2, 128), F32)
    info[0] = jnp.concatenate([ids[...].astype(F32), zero, weight[...], targets[...].astype(F32), zero[0:1]], axis=0)
    for own in owns:
        own.wait()
    for load in loads + [again]:
        load.start()
    pl.semaphore_wait(barrier, 22)
    swaps = [remote(src, dst, wsend.at[i], wrecv.at[i], sibling) for i, (src, dst) in enumerate(moves)]

    def tell(r, _):
        remote(info.at[0], info.at[r], isend, irecv, plane_peer(co, r)).start()
        return 0

    lax.fori_loop(1, 16, tell, 0)
    for s in swaps:
        s.start()
    sc_first, sc_second, sc_third = scatter_rings(part, land_c, land_b, land_a, co, sc_send, sc_recv)

    def routes():
        others = info.at[pl.ds(1, 15)]
        pltpu.make_async_copy(others, others, irecv).wait()
        pltpu.make_async_copy(others, others, isend).wait()

        def read_source(q, _):
            got_info = info[(q_me - q + 16) % 16]
            named, by = got_info[0:6], got_info[8:14]
            mask_rows, gate_rows = [], []
            for l in range(4):
                hit = named == (4 * q_me + l).astype(F32)
                mask_rows.append(jnp.sum(jnp.where(hit, 1.0, 0.0), axis=0, keepdims=True))
                gate_rows.append(jnp.sum(jnp.where(hit, by, 0.0), axis=0, keepdims=True))
            none = jnp.zeros((4, 128), F32)
            at = pl.ds(pl.multiple_of(q * 8, 8), 8)
            masks[at] = jnp.concatenate(mask_rows + [none], axis=0)
            gates[at] = jnp.concatenate(gate_rows + [none], axis=0)
            goals[q] = jnp.transpose(jnp.broadcast_to(got_info[14:15], (128, 128)))
            return 0

        lax.fori_loop(0, 16, read_source, 0)
        before = (
            lax.broadcasted_iota(jnp.int32, (128, 128), 0) < lax.broadcasted_iota(jnp.int32, (128, 128), 1)
        ).astype(F32).astype(BF)
        taken = masks[...]
        ahead = jnp.dot(taken.astype(BF), before, preferred_element_type=F32)
        places[...] = jnp.where(taken > 0.0, ahead, -1.0)

        def picking(p, _):
            slot = lax.broadcasted_iota(jnp.int32, (24, 128), 0).astype(F32)
            none = jnp.zeros((24, 128), F32)
            at = pl.ds(pl.multiple_of(p * 16, 16), 16)
            place, by = places[at], gates[at]
            pick = []
            for l in range(4):
                for s in range(2):
                    k = s * 8 + l
                    hit = jnp.where(place[k : k + 1] == slot, 1.0, 0.0)
                    pick.append(jnp.concatenate([hit, none] if s == 0 else [none, hit], axis=1))
                    row_gate[l, pl.ds(pl.multiple_of(p * 48 + s * 24, 8), 24)] = jnp.sum(
                        hit * by[k : k + 1], axis=1, keepdims=True
                    )
            picks[p] = jnp.concatenate(pick, axis=0).astype(BF)
            return 0

        lax.fori_loop(0, 8, picking, 0)
        for i in range(3):
            loads[i].wait()
            swaps[i].wait()

    def experts(j, half_way=None):
        if j not in (LEFT, FAR):
            if half_way:
                half_way()
            return
        pair = (OWN, LEFT) if j == LEFT else (RIGHT, FAR)
        ys = [shift(co, "y", GROUPS[k]) for k in pair]

        def place_of(t):
            return jnp.where(t < 2, ys[0], ys[1]), t % 2

        def select(t, _):
            y, i = place_of(t)
            two = buf[y, pl.ds(2 * i, 2)].reshape(256, 2048)
            chosen = jnp.dot(picks[2 * y + i], two, preferred_element_type=F32).astype(BF)
            for l in range(4):
                rows[l, pl.ds(pl.multiple_of(t * 48, 16), 48)] = chosen[l * 48 : (l + 1) * 48]
            return 0

        lax.fori_loop(0, 4, select, 0)

        def ffn(l, _):
            @pl.when(l == 2)
            def _():
                if j == LEFT:
                    half_way()
                else:
                    for n in (0, 1):
                        sc_first[n][OWN].forward()

            if j == FAR:

                @pl.when(l == 3)
                def _():
                    for n in (0, 1):
                        sc_first[n][LEFT].forward()

            both = lax.dot_general(rows[l], vgu[l], (((1,), (1,)), ((), ())), preferred_element_type=F32)
            gate, up = both[:, 0:352], both[:, 352:704]
            hidden = (gate / (1.0 + jnp.exp(-gate)) * up).astype(BF)
            scale = jnp.concatenate([row_gate[l, pl.ds(pl.multiple_of(y * 96, 8), 96)] for y in ys], axis=0)
            rows[l] = (jnp.dot(hidden, vd[l], preferred_element_type=F32) * scale).astype(BF)
            return 0

        lax.fori_loop(0, 4, ffn, 0)

        def combine(t, _):
            y, i = place_of(t)
            at = pl.ds(pl.multiple_of(t * 48, 16), 48)
            shares = jnp.concatenate([rows[l, at] for l in range(4)], axis=0)
            mixed = lax.dot_general(picks[2 * y + i], shares, (((0,), (0,)), ((), ())), preferred_element_type=F32)
            part[y, pl.ds(2 * i, 2)] = mixed.astype(BF).reshape(2, 4, 32, 2048)
            return 0

        lax.fori_loop(0, 4, combine, 0)
        for n in (0, 1):
            for k in (OWN, LEFT) if j == LEFT else (FAR, RIGHT):
                sc_first[n][k].start()

    lines = gather_groups(buf, co, ga_send.at[0], ga_recv.at[0], True, routes, experts)
    drain(buf, ga_send.at[0], COLORS, co, lines)
    for j in (FAR, LEFT, RIGHT, OWN):
        sc_first[2][j].start()
    for n in (0, 1, 2):
        sc_first[n][FAR].forward()
    sc_first[2][LEFT].forward()
    for n in (0, 1):
        sc_first[n][RIGHT].forward()
    for n in (0, 1, 2):
        sc_first[n][FAR].finish()
        sc_second[n].start()
    sc_first[2][RIGHT].forward()
    sc_first[2][OWN].forward()
    for n in (0, 1, 2):
        sc_first[n][LEFT].finish()
        sc_first[n][RIGHT].finish()
        sc_second[n].forward()
    for n in (0, 1, 2):
        sc_first[n][OWN].finish()
    for n in (0, 1, 2):
        sc_second[n].finish()
        sc_third[n].start()
    for n in (0, 1, 2):
        sc_third[n].finish()
    again.wait()
    resid = (mine[...].astype(F32) + part[co["y"], co["z"], co["x"]].astype(F32)).astype(BF).astype(F32)
    square = jnp.mean(resid * resid, axis=1, keepdims=True)
    buf[co["y"], co["z"], co["x"]] = (resid * lax.rsqrt(square + 1e-06) * gain[...]).astype(BF)

    def words_ready():
        loads[3].wait()
        swaps[3].wait()
        drain(part, sc_send, BACK, co, range(3))

    def head(j, half_way=None):
        y = shift(co, "y", GROUPS[j])

        def pair(i, _):
            if half_way:
                pl.when(i == 1)(half_way)

            lane = lax.broadcasted_iota(jnp.int32, (128, 128), 1)
            column = lax.broadcasted_iota(jnp.int32, (256, 768), 1)
            two = buf[y, pl.ds(2 * i, 2)].reshape(256, 2048)
            q = 4 * y + 2 * i
            goal = jnp.concatenate([goals[q + s][:, 0:1] for s in range(2)], axis=0).astype(jnp.int32)
            logits = [jnp.dot(two, words[v], preferred_element_type=F32) for v in range(2)]
            top = jnp.maximum(*[jnp.max(value, axis=1, keepdims=True) for value in logits])
            total, chosen = 0.0, 0.0
            for v in range(2):
                base = ((q_me * 2 + v) * 4 + co["x"]) * 768
                total += jnp.sum(jnp.exp(logits[v] - top), axis=1, keepdims=True)
                chosen += jnp.sum(jnp.where(column == goal - base, logits[v], 0.0), axis=1, keepdims=True)
            norm = top + jnp.log(total)
            for s in range(2):
                at = slice(s * 128, (s + 1) * 128)
                both = jnp.where(lane == 0, norm[at], jnp.where(lane == 1, chosen[at], 0.0))
                stats[q + s] = jnp.transpose(both)[0:2]
            return 0

        lax.fori_loop(0, 2, pair, 0)

    def note(j, i):
        y, z, x = shift(co, "y", GROUPS[j]), (co["z"] + i // 4) % 4, (co["x"] + i) % 4
        slot = (GROUPS[j] % 4) * 16 + i
        return remote(stats.at[4 * y + z], got.at[slot], st_send, st_recv, device(co, y=y, z=z, x=x))

    def head_and_send(j, half_way=None):
        head(j, half_way)

        def send(i, _):
            note(j, i).start()
            return 0

        lax.fori_loop(1 if j == OWN else 0, 16, send, 0)

    lines = gather_groups(buf, co, ga_send.at[1], ga_recv.at[1], False, words_ready, head_and_send)
    got[0] = stats[q_me]
    drain(buf, ga_send.at[1], COLORS, co, lines)
    others = got.at[pl.ds(1, 63)]
    pltpu.make_async_copy(others, others, st_send).wait()
    pltpu.make_async_copy(others, others, st_recv).wait()
    norms = got[:, 0, :]
    best = jnp.max(norms, axis=0, keepdims=True)
    mass = jnp.sum(jnp.exp(norms - best), axis=0, keepdims=True)
    chosen = jnp.sum(got[:, 1, :], axis=0, keepdims=True)
    out[...] = chosen - best - jnp.log(mass)


def vmem(*shape, dtype=BF):
    return pltpu.VMEM(shape, dtype)


def body(tokens, expert_ids, gates, w_gate, w_up, w_down, norm_gain, lm_weight, targets):
    hbm, chip = pl.BlockSpec(memory_space=pl.ANY), pl.BlockSpec(memory_space=pltpu.VMEM)
    dma = pltpu.SemaphoreType.DMA
    out = pl.pallas_call(
        kernel,
        out_shape=jax.ShapeDtypeStruct((1, 128), F32),
        in_specs=[hbm, chip, chip, chip, hbm, hbm, hbm, chip, hbm],
        out_specs=chip,
        scratch_shapes=[
            vmem(4, 4, 4, 32, 2048), vmem(4, 704, 2048), vmem(4, 352, 2048), vmem(16, 16, 128, dtype=F32),
            vmem(4, 4, 4, 32, 2048), vmem(4, 3, 4, 32, 2048), vmem(3, 4, 32, 2048), vmem(3, 32, 2048),
            vmem(2, 2048, 768), vmem(32, 2048), vmem(16, 128, 128, dtype=F32),
            vmem(16, 2, 128, dtype=F32), vmem(64, 2, 128, dtype=F32),
            vmem(4, 192, 2048), vmem(8, 192, 256), vmem(4, 384, 1, dtype=F32),
            vmem(128, 128, dtype=F32), vmem(128, 128, dtype=F32), vmem(128, 128, dtype=F32),
            dma((2, 3, 3)), dma((2, 3, 6, 3)), dma((3, 3)), dma((3, 6, 3)), dma, dma,
            dma, dma, dma((4,)), dma((4,)), dma((15,)),
        ],
        compiler_params=pltpu.CompilerParams(collective_id=0, has_side_effects=True, vmem_limit_bytes=67043328),
        name="layer",
    )(
        tokens, expert_ids.T, gates.T, targets[None], jnp.swapaxes(w_gate, 1, 2), jnp.swapaxes(w_up, 1, 2), w_down,
        norm_gain[None], lm_weight,
    )
    return out[0]


def solution(mesh):
    in_specs = (
        P("expert", None),
        P("expert", None),
        P("expert", None),
        P("expert", None, "vocab"),
        P("expert", None, "vocab"),
        P("expert", "vocab", None),
        P(),
        P(None, ("expert", "vocab")),
        P("expert"),
    )
    return jax.shard_map(body, mesh=mesh, in_specs=in_specs, out_specs=P("expert"), check_vma=False)
```
